32 devices in a mesh: energy: 16 (over z, y, x), slab: 2 (over core).
Axes of the slice: x: 2, y: 2, z: 4, core: 2. Of those that a mesh axis runs over, the one named last changes fastest.
Arguments:
- green0: bfloat16 [16, 2, 2, 384, 384], P('energy', 'slab'), may hold values from -6 to 6
- coupling: bfloat16 [2, 3, 384, 384], P('slab'), may hold values from -0.09375 to 0.09375
Outputs:
- green: bfloat16 [16, 2, 2, 384, 384], P('energy', 'slab')
The draws below stay inside these ranges and needn't reach their ends.
All inputs are finite; a program needn't handle non-finite values.
Results may differ from the reference program's by a relative error of at most 0.012.
Values may be sent and summed in bfloat16 or wider, within the bound.
No kernel may reach another device: no remote copies, remote signals or barrier semaphores. Data moves between devices by JAX's collectives and lax.ppermute only.
A program may use at most 64 MiB of HBM per device.

```python
import jax
import jax.numpy as jnp
from jax import lax

B = 384
OFFSET = 7
ITERS = 2
ENERGIES = 16
SLABS = 2


def levels(own_key, dims, cuts, smallest, high):
    def one(axis_at, shards_of):
        heights = jax.random.uniform(jax.random.fold_in(jax.random.fold_in(own_key, 6), axis_at), (shards_of,), jnp.float32, smallest / len(cuts), high / len(cuts))
        return jnp.repeat(jnp.exp(heights), dims[axis_at] // shards_of).reshape((-1,) + (1,) * (len(dims) - axis_at - 1))

    level = one(*cuts[0])
    for cut in cuts[1:]:
        level = level * one(*cut)
    return level


def bell_draw(key, extent, width, most, cuts=(), held_as=jnp.bfloat16):
    drawn = width * jax.random.normal(key, extent, jnp.float32)
    if cuts:
        drawn = drawn * levels(key, extent, cuts, -0.22, 0.18)
    return jnp.clip(drawn, -most, most).astype(held_as)


def setup_inputs(seed: int = 0) -> dict:
    key_of = jax.random.split(jax.random.key(seed), 3)
    return {
        "green0": bell_draw(key_of[0], (ENERGIES, SLABS, 2, B, B), 1.0, 6.0, ((0, 16), (1, 2))),
        "coupling": bell_draw(key_of[1], (SLABS, 3, B, B), (10 * B) ** -0.5, 0.09375, ((0, 2),)),
    }


def mult(form, left, right):
    return jnp.einsum(form, left.astype(jnp.float32), right.astype(jnp.float32), precision=lax.Precision.HIGHEST)


def dyson(green0, coupling, summed):
    count = green0.shape[0]
    sigma = jnp.zeros(green0.shape, jnp.float32)
    for index in range(3):
        part = summed[index:index + count]
        weights = coupling[:, index]
        left = mult("sij,scjk->scik", weights, part).astype(jnp.bfloat16)
        sigma = sigma + mult("scij,skj->scik", left, weights)
    sigma = sigma.astype(jnp.bfloat16)
    green_re = green0[:, 0]
    green_im = green0[:, 1]
    prod_re = mult("sij,sjk->sik", green_re, sigma[:, 0]) - mult("sij,sjk->sik", green_im, sigma[:, 1])
    prod_im = mult("sij,sjk->sik", green_re, sigma[:, 1]) + mult("sij,sjk->sik", green_im, sigma[:, 0])
    prod_re = prod_re.astype(jnp.bfloat16)
    prod_im = prod_im.astype(jnp.bfloat16)
    out_re = mult("sij,skj->sik", prod_re, green_re) - mult("sij,skj->sik", prod_im, green_im)
    out_im = mult("sij,skj->sik", prod_re, green_im) + mult("sij,skj->sik", prod_im, green_re)
    result = green0.astype(jnp.float32) + jnp.stack([out_re, out_im], axis=1) / B
    return result.astype(jnp.bfloat16)


def reference(green0, coupling):
    green = green0
    for turn in range(ITERS):
        empty = jnp.zeros((OFFSET,) + green.shape[1:], jnp.bfloat16)
        lower = jnp.concatenate([empty, green[:-OFFSET]], axis=0)
        upper = jnp.concatenate([green[OFFSET:], empty], axis=0)
        both = (lower.astype(jnp.float32) + upper.astype(jnp.float32)).astype(jnp.bfloat16)
        summed = jnp.pad(both, ((0, 0), (1, 1), (0, 0), (0, 0), (0, 0)))
        green = lax.map(lambda pair: dyson(pair[0], coupling, pair[1]), (green0, summed))
    return green
```

```python
import functools

import jax
import jax.numpy as jnp
from jax import lax
from jax.experimental import pallas as pl
from jax.experimental.pallas import tpu as pltpu
from jax.sharding import PartitionSpec as P

OFFSET = 7
ITERS = 2
VMEM_LIMIT = 12 << 20
LAYER = 4


def passed_along(value, axis, steps):
    count = lax.axis_size(axis)
    first, last = (max(0, -steps), min(count, count - steps))
    return lax.ppermute(value, axis, [(source, source + steps) for source in range(first, last)])


def with_halo(block, sides, width):
    for axis, dim in sides:
        count = lax.axis_size(axis)
        forward = [(i, i + 1) for i in range(count - 1)]
        backward = [(target, source) for source, target in forward]
        low = lax.ppermute(
            lax.slice_in_dim(block, block.shape[dim] - width, None, axis=dim), axis, forward
        )
        high = lax.ppermute(lax.slice_in_dim(block, 0, width, axis=dim), axis, backward)
        block = jnp.concatenate([low, block, high], axis=dim)
    return block


def dyson(green0, coupling, summed):
    count = green0.shape[1]
    size = green0.shape[-1]
    sigma = jnp.zeros(green0.shape, jnp.float32)
    for index in range(3):
        part = summed[:, index : index + count]
        weights = coupling[:, index]
        left = jnp.einsum(
            "sij,escjk->escik", weights, part, preferred_element_type=jnp.float32
        ).astype(jnp.bfloat16)
        sigma = sigma + jnp.einsum(
            "escij,skj->escik", left, weights, preferred_element_type=jnp.float32
        )
    sigma = sigma.astype(jnp.bfloat16)
    green_re = green0[:, :, 0]
    green_im = green0[:, :, 1]
    form = "esij,esjk->esik"
    prod_re = jnp.einsum(
        form, green_re, sigma[:, :, 0], preferred_element_type=jnp.float32
    ) - jnp.einsum(form, green_im, sigma[:, :, 1], preferred_element_type=jnp.float32)
    prod_im = jnp.einsum(
        form, green_re, sigma[:, :, 1], preferred_element_type=jnp.float32
    ) + jnp.einsum(form, green_im, sigma[:, :, 0], preferred_element_type=jnp.float32)
    prod_re = prod_re.astype(jnp.bfloat16)
    prod_im = prod_im.astype(jnp.bfloat16)
    trans = "esij,eskj->esik"
    out_re = jnp.einsum(trans, prod_re, green_re, preferred_element_type=jnp.float32) - jnp.einsum(
        trans, prod_im, green_im, preferred_element_type=jnp.float32
    )
    out_im = jnp.einsum(trans, prod_re, green_im, preferred_element_type=jnp.float32) + jnp.einsum(
        trans, prod_im, green_re, preferred_element_type=jnp.float32
    )
    result = green0.astype(jnp.float32) + jnp.stack([out_re, out_im], axis=2) / size
    return result.astype(jnp.bfloat16)


def plain(green0, coupling):
    green = green0
    for turn in range(ITERS):
        lower = passed_along(green, "energy", OFFSET)
        upper = passed_along(green, "energy", -OFFSET)
        own_sum = (lower.astype(jnp.float32) + upper.astype(jnp.float32)).astype(jnp.bfloat16)
        summed = with_halo(own_sum, (("slab", 1),), 1)
        green = dyson(green0, coupling, summed)
    return green


def routes(energies):
    chains = [list(range(first, energies, OFFSET)) for first in range(min(OFFSET, energies))]
    threes = [chain for chain in chains if len(chain) == 3]
    twos = [chain for chain in chains if len(chain) == 2]

    def crossing(one, two):
        spans = [sorted((end // LAYER for end in flow)) for flow in (one, two)]
        same_way = (one[1] > one[0]) == (two[1] > two[0])
        over = max(spans[0][0], spans[1][0]) < min(spans[0][1], spans[1][1])
        return same_way and over and one[0] % LAYER == two[0] % LAYER

    lower = [(low, mid) for low, mid, _ in threes]
    upper = [(high, mid) for _, mid, high in threes]
    pairs = [flow for a, b in twos for flow in ((a, b), (b, a))]
    late = [flow for flow in pairs if any(crossing(flow, into) for into in lower + upper)]
    first = lower + [flow for flow in pairs if flow not in late]
    back = ([(mid, high) for _, mid, high in threes], [(mid, low) for low, mid, _ in threes])
    return first, upper, late, back


def dot(left, right):
    return jnp.dot(left, right, preferred_element_type=jnp.float32)


def dot_t(left, right):
    return lax.dot_general(
        left, right, (((1,), (1,)), ((), ())), preferred_element_type=jnp.float32
    )


def self_energy(mine, other, weights, beside):
    size = mine.shape[-1]
    own, far = weights[1], weights[beside]
    near = dot(own, jnp.concatenate([mine[0], mine[1]], axis=1)).astype(jnp.bfloat16)
    cross = dot(far, jnp.concatenate([other[0], other[1]], axis=1)).astype(jnp.bfloat16)
    left = jnp.concatenate(
        [
            jnp.concatenate([near[:, :size], cross[:, :size]], axis=1),
            jnp.concatenate([near[:, size:], cross[:, size:]], axis=1),
        ],
        axis=0,
    )
    return dot_t(left, jnp.concatenate([own, far], axis=1)).astype(jnp.bfloat16)


def stepped(green, sigma_re, sigma_im):
    re, im = green[0], green[1]
    size = re.shape[0]
    square = jnp.concatenate(
        [
            jnp.concatenate([sigma_re, sigma_im], axis=1),
            jnp.concatenate([-sigma_im, sigma_re], axis=1),
        ],
        axis=0,
    )
    product = dot(jnp.concatenate([re, im], axis=1), square).astype(jnp.bfloat16)
    turned = jnp.concatenate(
        [jnp.concatenate([re, -im], axis=1), jnp.concatenate([im, re], axis=1)], axis=0
    )
    added = dot_t(product, turned)
    return (
        re.astype(jnp.float32) + added[:, :size] / size,
        im.astype(jnp.float32) + added[:, size:] / size,
    )


def sigma_kernel(flags, mine, other, weights, out):
    size = mine.shape[-1]
    sigma = self_energy(mine, other, weights, flags[0])
    out[0] = sigma[:size]
    out[1] = sigma[size:]


def sum_kernel(flags, one, two, out):
    @pl.when(flags[1] == 1)
    def _():
        out[...] = (one[...].astype(jnp.float32) + two[...].astype(jnp.float32)).astype(out.dtype)


def pick_kernel(flags, stepped_on, high, low, out):
    for value, source in enumerate((stepped_on, high, low)):

        @pl.when(flags[4] == value)
        def _():
            out[...] = source[...]


def centre_kernel(flags, own, mine, other, weights, out):
    @pl.when(flags[1] == 1)
    def _():
        size = own.shape[-1]
        sigma = self_energy(mine, other, weights, flags[0])
        out[0], out[1] = (
            part.astype(jnp.bfloat16) for part in stepped(own, sigma[:size], sigma[size:])
        )


def neighbour_kernel(flags, first, upper, late, sigma, out):
    @pl.when(flags[1] == 1)
    def _():
        below = stepped(first, sigma[0], sigma[1])
        above = stepped(upper, sigma[0], sigma[1])
        for part in range(2):
            one = below[part].astype(jnp.bfloat16).astype(jnp.float32)
            two = above[part].astype(jnp.bfloat16).astype(jnp.float32)
            out[part] = (one + two).astype(jnp.bfloat16)

    for flag, source in ((2, first), (3, late)):

        @pl.when(flags[flag] == 1)
        def _():
            out[0], out[1] = (
                part.astype(jnp.bfloat16) for part in stepped(source, sigma[0], sigma[1])
            )


def last_kernel(flags, own, mine, other, weights, out):
    size = own.shape[-1]
    sigma = self_energy(mine, other, weights, flags[0])
    out[0], out[1] = (
        part.astype(jnp.bfloat16) for part in stepped(own, sigma[:size], sigma[size:])
    )


def call(kernel, flags, *blocks):
    like = blocks[0]
    return pl.pallas_call(
        kernel,
        out_shape=jax.ShapeDtypeStruct(like.shape, like.dtype),
        in_specs=[pl.BlockSpec(memory_space=pltpu.SMEM)]
        + [pl.BlockSpec(memory_space=pltpu.VMEM)] * len(blocks),
        out_specs=pl.BlockSpec(memory_space=pltpu.VMEM),
        compiler_params=pltpu.CompilerParams(vmem_limit_bytes=VMEM_LIMIT),
        name=kernel.__name__,
    )(flags, *blocks)


def chained(first, upper, late, back, green0, coupling):
    own, weights = green0[0, 0], coupling[0]
    energy, slab = lax.axis_index("energy"), lax.axis_index("slab")
    slabs = lax.axis_size("slab")

    def is_in(members):
        return functools.reduce(
            jnp.logical_or, [energy == member for member in members], jnp.bool_(False)
        ).astype(jnp.int32)

    middles = [target for _, target in upper]
    flags = jnp.stack(
        [
            jnp.where(slab == 0, 2, 0).astype(jnp.int32),
            is_in(middles),
            is_in([target for _, target in first if target not in middles]),
            is_in([target for _, target in late]),
            sum(is_in([target for _, target in flows]) * (i + 1) for i, flows in enumerate(back)),
        ]
    )

    def swapped(value, members):
        flows = [(i * slabs + s, i * slabs + 1 - s) for i in members for s in range(slabs)]
        return lax.ppermute(value, ("energy", "slab"), flows)

    everyone = range(lax.axis_size("energy"))
    from_first = lax.ppermute(own, "energy", first)
    from_upper = lax.ppermute(own, "energy", upper)
    sigma = call(sigma_kernel, flags, own, swapped(own, everyone), weights)
    from_first, from_upper, sigma, held = lax.optimization_barrier(
        (from_first, from_upper, sigma, own)
    )
    from_late = lax.ppermute(held, "energy", late)
    both = call(sum_kernel, flags, from_first, from_upper)
    centre = call(centre_kernel, flags, own, both, swapped(both, middles), weights)
    returned = [lax.ppermute(centre, "energy", flows) for flows in back]
    stepped_on = call(neighbour_kernel, flags, from_first, from_upper, from_late, sigma)
    green = call(pick_kernel, flags, stepped_on, *returned)
    out = call(last_kernel, flags, own, green, swapped(green, everyone), weights)
    return out[None, None]


def solution(mesh):
    energies, slabs = mesh.shape["energy"], mesh.shape["slab"]
    if OFFSET < energies <= 3 * OFFSET and slabs == 2:
        local = functools.partial(chained, *routes(energies))
    else:
        local = plain
    placed = (P("energy", "slab", None, None, None), P("slab", None, None, None))
    return jax.shard_map(
        local,
        mesh=mesh,
        in_specs=placed,
        out_specs=P("energy", "slab", None, None, None),
        check_vma=False,
    )
```

```python
import functools

import jax
import jax.numpy as jnp
from jax import lax
from jax.experimental import pallas as pl
from jax.experimental.pallas import tpu as pltpu
from jax.sharding import PartitionSpec as P

OFFSET = 7
ITERS = 2
VMEM_LIMIT = 12 << 20
ROW, LAYER = 2, 4


def passed_along(value, axis, steps):
    count = lax.axis_size(axis)
    first, last = (max(0, -steps), min(count, count - steps))
    return lax.ppermute(value, axis, [(source, source + steps) for source in range(first, last)])


def with_halo(block, sides, width):
    for axis, dim in sides:
        count = lax.axis_size(axis)
        forward = [(i, i + 1) for i in range(count - 1)]
        backward = [(target, source) for source, target in forward]
        low = lax.ppermute(
            lax.slice_in_dim(block, block.shape[dim] - width, None, axis=dim), axis, forward
        )
        high = lax.ppermute(lax.slice_in_dim(block, 0, width, axis=dim), axis, backward)
        block = jnp.concatenate([low, block, high], axis=dim)
    return block


def dyson(green0, coupling, summed):
    count = green0.shape[1]
    size = green0.shape[-1]
    sigma = jnp.zeros(green0.shape, jnp.float32)
    for index in range(3):
        part = summed[:, index : index + count]
        weights = coupling[:, index]
        left = jnp.einsum(
            "sij,escjk->escik", weights, part, preferred_element_type=jnp.float32
        ).astype(jnp.bfloat16)
        sigma = sigma + jnp.einsum(
            "escij,skj->escik", left, weights, preferred_element_type=jnp.float32
        )
    sigma = sigma.astype(jnp.bfloat16)
    green_re = green0[:, :, 0]
    green_im = green0[:, :, 1]
    form = "esij,esjk->esik"
    prod_re = jnp.einsum(
        form, green_re, sigma[:, :, 0], preferred_element_type=jnp.float32
    ) - jnp.einsum(form, green_im, sigma[:, :, 1], preferred_element_type=jnp.float32)
    prod_im = jnp.einsum(
        form, green_re, sigma[:, :, 1], preferred_element_type=jnp.float32
    ) + jnp.einsum(form, green_im, sigma[:, :, 0], preferred_element_type=jnp.float32)
    prod_re = prod_re.astype(jnp.bfloat16)
    prod_im = prod_im.astype(jnp.bfloat16)
    trans = "esij,eskj->esik"
    out_re = jnp.einsum(trans, prod_re, green_re, preferred_element_type=jnp.float32) - jnp.einsum(
        trans, prod_im, green_im, preferred_element_type=jnp.float32
    )
    out_im = jnp.einsum(trans, prod_re, green_im, preferred_element_type=jnp.float32) + jnp.einsum(
        trans, prod_im, green_re, preferred_element_type=jnp.float32
    )
    result = green0.astype(jnp.float32) + jnp.stack([out_re, out_im], axis=2) / size
    return result.astype(jnp.bfloat16)


def plain(green0, coupling):
    green = green0
    for _ in range(ITERS):
        lower = passed_along(green, "energy", OFFSET)
        upper = passed_along(green, "energy", -OFFSET)
        own_sum = (lower.astype(jnp.float32) + upper.astype(jnp.float32)).astype(jnp.bfloat16)
        summed = with_halo(own_sum, (("slab", 1),), 1)
        green = dyson(green0, coupling, summed)
    return green


def links(source, target):
    passed, at = [], source
    for step, size in ((LAYER, None), (1, ROW), (ROW, LAYER)):
        here, there = ((e // step if size is None else e % size // step) for e in (at, target))
        for _ in range(abs(there - here)):
            to = at + (step if there > here else -step)
            passed.append((at, to))
            at = to
    return passed


def planned(energies):
    chains = [list(range(first, energies, OFFSET)) for first in range(min(OFFSET, energies))]
    threes = [chain for chain in chains if len(chain) == 3]
    twos = [chain for chain in chains if len(chain) == 2]
    if len(threes) != 2 or len(threes) + len(twos) != len(chains):
        return None
    (low0, mid0, high0), (low1, mid1, high1) = threes
    inward = [(low0, mid0), (low1, mid1), (high0, mid0), (high1, mid1)]
    plan = {
        "first": inward[:2],
        "other": inward[2:],
        "ends": [(low0, low1), (low1, low0), (high0, high1), (high1, high0)],
        "second": [(mid0, low0), (mid1, low1), (low0, mid1), (low1, mid0)],
        "third": [(mid0, high0), (mid1, high1)],
        "inner": [(high0, mid1), (high1, mid0)],
    }
    busy = {link for flow in inward for link in links(*flow)}
    taken = {link for flow in plan["ends"] for link in links(*flow)}
    direct, late, relays = [], [], []
    for source, target in [flow for a, b in twos for flow in ((a, b), (b, a))]:
        passed = set(links(source, target))
        relay = target - target % LAYER + source % LAYER
        if passed & taken or any(abs(a - b) == LAYER for a, b in passed & busy):
            plan["second"].append((source, target))
            late.append((source, target))
        elif passed & busy:
            plan["other"].append((source, relay))
            plan["second"].append((relay, target))
            relays.append((relay, target))
            taken |= set(links(source, relay))
        else:
            plan["first"].append((source, target))
            direct.append(target)
            taken |= passed
    for flows in plan.values():
        sources, targets = zip(*flows)
        if len(set(sources)) < len(flows) or len(set(targets)) < len(flows):
            return None
    plan["lows"], plan["mids"], plan["highs"] = ([a, b] for a, b in zip(*threes))
    plan["direct"] = direct
    plan["relayed"] = [relay for relay, _ in relays]
    plan["late"] = [source for source, _ in late]
    plan["second_pairs"] = [target for _, target in late + relays]
    return plan


def dot(left, right):
    return jnp.dot(left, right, preferred_element_type=jnp.float32)


def dot_t(left, right):
    return lax.dot_general(
        left, right, (((1,), (1,)), ((), ())), preferred_element_type=jnp.float32
    )


def among(members):
    energy = lax.axis_index("energy")
    return functools.reduce(jnp.logical_or, [energy == member for member in members])


def self_energy(mine, other, weights):
    size = mine.shape[-1]
    own, far = weights[1], weights[2 - 2 * lax.axis_index("slab")]
    near = dot(own, jnp.concatenate([mine[0], mine[1]], axis=1)).astype(jnp.bfloat16)
    cross = dot(far, jnp.concatenate([other[0], other[1]], axis=1)).astype(jnp.bfloat16)
    left = jnp.concatenate(
        [
            jnp.concatenate([near[:, :size], cross[:, :size]], axis=1),
            jnp.concatenate([near[:, size:], cross[:, size:]], axis=1),
        ],
        axis=0,
    )
    return dot_t(left, jnp.concatenate([own, far], axis=1)).astype(jnp.bfloat16)


def stepped(green, sigma_re, sigma_im):
    re, im = green[0], green[1]
    size = re.shape[0]
    square = jnp.concatenate(
        [
            jnp.concatenate([sigma_re, sigma_im], axis=1),
            jnp.concatenate([-sigma_im, sigma_re], axis=1),
        ],
        axis=0,
    )
    product = dot(jnp.concatenate([re, im], axis=1), square).astype(jnp.bfloat16)
    turned = jnp.concatenate(
        [jnp.concatenate([re, -im], axis=1), jnp.concatenate([im, re], axis=1)], axis=0
    )
    added = dot_t(product, turned)
    return (
        re.astype(jnp.float32) + added[:, :size] / size,
        im.astype(jnp.float32) + added[:, size:] / size,
    )


def put(out, parts):
    for part, value in enumerate(parts):
        out[part] = value.astype(out.dtype)


def added(one, two):
    return (one.astype(jnp.float32) + two.astype(jnp.float32)).astype(one.dtype)


def load_kernel(own, weights, own_out, weights_out, sems):
    copies = [
        pltpu.make_async_copy(own, own_out, sems.at[0]),
        pltpu.make_async_copy(weights, weights_out, sems.at[1]),
    ]
    for copy in copies:
        copy.start()
    for copy in copies:
        copy.wait()


def loaded(*blocks):
    return pl.pallas_call(
        load_kernel,
        out_shape=[jax.ShapeDtypeStruct(block.shape, block.dtype) for block in blocks],
        in_specs=[pl.BlockSpec(memory_space=pltpu.HBM)] * len(blocks),
        out_specs=[pl.BlockSpec(memory_space=pltpu.VMEM)] * len(blocks),
        scratch_shapes=[pltpu.SemaphoreType.DMA((len(blocks),))],
        compiler_params=pltpu.CompilerParams(vmem_limit_bytes=VMEM_LIMIT),
        name="load_kernel",
    )(*(pltpu.with_memory_space_constraint(block, pltpu.HBM) for block in blocks))


def first_kernel(plan, own, beside, weights, send):
    size = own.shape[-1]
    is_end = among(plan["lows"] + plan["highs"])

    @pl.when(is_end)
    def _():
        sigma = self_energy(own, beside, weights)
        send[0] = sigma[:size]
        send[1] = sigma[size:]

    @pl.when(jnp.logical_not(is_end))
    def _():
        send[...] = own[...]


def sigma_kernel(plan, own, beside, weights, sigma_out):
    size = own.shape[-1]

    @pl.when(jnp.logical_not(among(plan["lows"] + plan["highs"])))
    def _():
        sigma = self_energy(own, beside, weights)
        sigma_out[0] = sigma[:size]
        sigma_out[1] = sigma[size:]


def second_kernel(plan, own, first, other, ends, send):
    @pl.when(among(plan["mids"]))
    def _():
        sigma = [added(first[part], other[part]) for part in range(2)]
        put(send, stepped(own, *sigma))

    for members, source in (
        (plan["relayed"], other),
        (plan["late"], own),
        (plan["lows"], ends),
    ):

        @pl.when(among(members))
        def _():
            send[...] = source[...]


def neighbour_kernel(plan, first, second, third, inner, sigma, out):
    @pl.when(among(plan["mids"]))
    def _():
        steps = [stepped(block, sigma[0], sigma[1]) for block in (second, inner)]
        put(out, [added(*(step[part].astype(out.dtype) for step in steps)) for part in range(2)])

    for members, source in ((plan["direct"], first), (plan["second_pairs"], second)):

        @pl.when(among(members))
        def _():
            put(out, stepped(source, sigma[0], sigma[1]))

    for members, source in ((plan["lows"], second), (plan["highs"], third)):

        @pl.when(among(members))
        def _():
            out[...] = source[...]


def last_kernel(plan, own, mine, other, weights, out):
    size = own.shape[-1]
    sigma = self_energy(mine, other, weights)
    put(out, stepped(own, sigma[:size], sigma[size:]))


def call(kernel, plan, *blocks):
    space = pl.BlockSpec(memory_space=pltpu.VMEM)
    return pl.pallas_call(
        functools.partial(kernel, plan),
        out_shape=jax.ShapeDtypeStruct(blocks[0].shape, blocks[0].dtype),
        in_specs=[space] * len(blocks),
        out_specs=space,
        compiler_params=pltpu.CompilerParams(vmem_limit_bytes=VMEM_LIMIT),
    )(*blocks)


def chained(plan, green0, coupling):
    own, weights = green0[0, 0], coupling[0]
    slabs = lax.axis_size("slab")

    def sent(value, flows):
        return lax.ppermute(value, "energy", plan[flows])

    def swapped(value):
        return lax.ppermute(value, "slab", [(s, slabs - 1 - s) for s in range(slabs)])

    beside = swapped(own)
    own, weights = loaded(own, weights)
    send = call(first_kernel, plan, own, beside, weights)
    ends, other, first = sent(own, "ends"), sent(send, "other"), sent(send, "first")
    inner = sent(ends, "inner")
    sigma = call(sigma_kernel, plan, own, beside, weights)
    send = call(second_kernel, plan, own, first, other, ends)
    second, third = sent(send, "second"), sent(send, "third")
    green = call(neighbour_kernel, plan, first, second, third, inner, sigma)
    out = call(last_kernel, plan, own, green, swapped(green), weights)
    return out[None, None]


def solution(mesh):
    plan = planned(mesh.shape["energy"]) if mesh.shape["slab"] == 2 else None
    local = functools.partial(chained, plan) if plan else plain
    placed = (P("energy", "slab", None, None, None), P("slab", None, None, None))
    return jax.shard_map(
        local,
        mesh=mesh,
        in_specs=placed,
        out_specs=P("energy", "slab", None, None, None),
        check_vma=False,
    )
```

```python
import functools

import jax
import jax.numpy as jnp
from jax import lax
from jax.experimental import pallas as pl
from jax.experimental.pallas import tpu as pltpu
from jax.sharding import PartitionSpec as P

OFFSET = 7
ITERS = 2
VMEM_LIMIT = 12 << 20
ROW, LAYER = 2, 4


def passed_along(value, axis, steps):
    count = lax.axis_size(axis)
    first, last = (max(0, -steps), min(count, count - steps))
    return lax.ppermute(value, axis, [(source, source + steps) for source in range(first, last)])


def with_halo(block, sides, width):
    for axis, dim in sides:
        count = lax.axis_size(axis)
        forward = [(i, i + 1) for i in range(count - 1)]
        backward = [(target, source) for source, target in forward]
        low = lax.ppermute(
            lax.slice_in_dim(block, block.shape[dim] - width, None, axis=dim), axis, forward
        )
        high = lax.ppermute(lax.slice_in_dim(block, 0, width, axis=dim), axis, backward)
        block = jnp.concatenate([low, block, high], axis=dim)
    return block


def dyson(green0, coupling, summed):
    count = green0.shape[1]
    size = green0.shape[-1]
    sigma = jnp.zeros(green0.shape, jnp.float32)
    for index in range(3):
        part = summed[:, index : index + count]
        weights = coupling[:, index]
        left = jnp.einsum(
            "sij,escjk->escik", weights, part, preferred_element_type=jnp.float32
        ).astype(jnp.bfloat16)
        sigma = sigma + jnp.einsum(
            "escij,skj->escik", left, weights, preferred_element_type=jnp.float32
        )
    sigma = sigma.astype(jnp.bfloat16)
    green_re = green0[:, :, 0]
    green_im = green0[:, :, 1]
    form = "esij,esjk->esik"
    prod_re = jnp.einsum(
        form, green_re, sigma[:, :, 0], preferred_element_type=jnp.float32
    ) - jnp.einsum(form, green_im, sigma[:, :, 1], preferred_element_type=jnp.float32)
    prod_im = jnp.einsum(
        form, green_re, sigma[:, :, 1], preferred_element_type=jnp.float32
    ) + jnp.einsum(form, green_im, sigma[:, :, 0], preferred_element_type=jnp.float32)
    prod_re = prod_re.astype(jnp.bfloat16)
    prod_im = prod_im.astype(jnp.bfloat16)
    trans = "esij,eskj->esik"
    out_re = jnp.einsum(trans, prod_re, green_re, preferred_element_type=jnp.float32) - jnp.einsum(
        trans, prod_im, green_im, preferred_element_type=jnp.float32
    )
    out_im = jnp.einsum(trans, prod_re, green_im, preferred_element_type=jnp.float32) + jnp.einsum(
        trans, prod_im, green_re, preferred_element_type=jnp.float32
    )
    result = green0.astype(jnp.float32) + jnp.stack([out_re, out_im], axis=2) / size
    return result.astype(jnp.bfloat16)


def plain(green0, coupling):
    green = green0
    for _ in range(ITERS):
        lower = passed_along(green, "energy", OFFSET)
        upper = passed_along(green, "energy", -OFFSET)
        own_sum = (lower.astype(jnp.float32) + upper.astype(jnp.float32)).astype(jnp.bfloat16)
        summed = with_halo(own_sum, (("slab", 1),), 1)
        green = dyson(green0, coupling, summed)
    return green


def links(source, target):
    passed, at = [], source
    for step, size in ((LAYER, None), (1, ROW), (ROW, LAYER)):
        here, there = ((e // step if size is None else e % size // step) for e in (at, target))
        for _ in range(abs(there - here)):
            to = at + (step if there > here else -step)
            passed.append((at, to))
            at = to
    return passed


def planned(energies):
    chains = [list(range(first, energies, OFFSET)) for first in range(min(OFFSET, energies))]
    threes = [chain for chain in chains if len(chain) == 3]
    twos = [chain for chain in chains if len(chain) == 2]
    if len(threes) != 2 or len(threes) + len(twos) != len(chains):
        return None
    (low0, mid0, high0), (low1, mid1, high1) = threes
    inward = [(low0, mid0), (low1, mid1), (high0, mid0), (high1, mid1)]
    plan = {
        "first": inward[:2],
        "other": inward[2:],
        "ends": [(low0, low1), (low1, low0), (high0, high1), (high1, high0)],
        "second": [(mid0, low0), (mid1, low1)],
        "third": [(mid0, high0), (mid1, high1)],
        "below": [(low0, mid1), (low1, mid0)],
        "above": [(high0, mid1), (high1, mid0)],
    }
    busy = {link for flow in inward for link in links(*flow)}
    taken = {link for flow in plan["ends"] for link in links(*flow)}
    direct, late, relays = [], [], []
    for source, target in [flow for a, b in twos for flow in ((a, b), (b, a))]:
        passed = set(links(source, target))
        relay = target - target % LAYER + source % LAYER
        if passed & taken or any(abs(a - b) == LAYER for a, b in passed & busy):
            plan["second"].append((source, target))
            late.append((source, target))
        elif passed & busy:
            plan["other"].append((source, relay))
            plan["second"].append((relay, target))
            relays.append((relay, target))
            taken |= set(links(source, relay))
        else:
            plan["first"].append((source, target))
            direct.append(target)
            taken |= passed
    for flows in plan.values():
        sources, targets = zip(*flows)
        if len(set(sources)) < len(flows) or len(set(targets)) < len(flows):
            return None
    plan["lows"], plan["mids"], plan["highs"] = ([a, b] for a, b in zip(*threes))
    plan["direct"] = direct
    plan["senders"] = [source for source, _ in plan["first"][2:] + plan["other"][2:]]
    plan["relayed"] = [relay for relay, _ in relays]
    plan["late"] = [source for source, _ in late]
    plan["second_pairs"] = [target for _, target in late + relays]
    return plan


def dot(left, right):
    return jnp.dot(left, right, preferred_element_type=jnp.float32)


def dot_t(left, right):
    return lax.dot_general(
        left, right, (((1,), (1,)), ((), ())), preferred_element_type=jnp.float32
    )


def among(members):
    energy = lax.axis_index("energy")
    return functools.reduce(jnp.logical_or, [energy == member for member in members])


def self_energy(mine, other, weights):
    size = mine.shape[-1]
    own, far = weights[1], weights[2 - 2 * lax.axis_index("slab")]
    near = dot(own, jnp.concatenate([mine[0], mine[1]], axis=1)).astype(jnp.bfloat16)
    cross = dot(far, jnp.concatenate([other[0], other[1]], axis=1)).astype(jnp.bfloat16)
    left = jnp.concatenate(
        [
            jnp.concatenate([near[:, :size], cross[:, :size]], axis=1),
            jnp.concatenate([near[:, size:], cross[:, size:]], axis=1),
        ],
        axis=0,
    )
    return dot_t(left, jnp.concatenate([own, far], axis=1)).astype(jnp.bfloat16)


def stepped(green, sigma_re, sigma_im):
    re, im = green[0], green[1]
    size = re.shape[0]
    square = jnp.concatenate(
        [
            jnp.concatenate([sigma_re, sigma_im], axis=1),
            jnp.concatenate([-sigma_im, sigma_re], axis=1),
        ],
        axis=0,
    )
    product = dot(jnp.concatenate([re, im], axis=1), square).astype(jnp.bfloat16)
    turned = jnp.concatenate(
        [jnp.concatenate([re, -im], axis=1), jnp.concatenate([im, re], axis=1)], axis=0
    )
    added = dot_t(product, turned)
    return (
        re.astype(jnp.float32) + added[:, :size] / size,
        im.astype(jnp.float32) + added[:, size:] / size,
    )


def put(out, parts):
    for part, value in enumerate(parts):
        out[part] = value.astype(out.dtype)


def added(one, two):
    return (one.astype(jnp.float32) + two.astype(jnp.float32)).astype(one.dtype)


def load_kernel(own, weights, own_out, weights_out, sems):
    copies = [
        pltpu.make_async_copy(own, own_out, sems.at[0]),
        pltpu.make_async_copy(weights, weights_out, sems.at[1]),
    ]
    for copy in copies:
        copy.start()
    for copy in copies:
        copy.wait()


def first_kernel(plan, own, beside, weights, send, held, sems):
    size = own.shape[-1]

    @pl.when(among(plan["lows"] + plan["highs"]))
    def _():
        blocks, rows = held
        copies = [
            pltpu.make_async_copy(own, blocks, sems.at[0]),
            pltpu.make_async_copy(weights, rows, sems.at[1]),
        ]
        for copy in copies:
            copy.start()
        for copy in copies:
            copy.wait()
        sigma = self_energy(blocks, beside, rows)
        send[0] = sigma[:size]
        send[1] = sigma[size:]

    @pl.when(among(plan["senders"]))
    def _():
        copy = pltpu.make_async_copy(own, send, sems.at[0])
        copy.start()
        copy.wait()


def sigma_kernel(plan, own, beside, weights, sigma_out):
    size = own.shape[-1]

    @pl.when(jnp.logical_not(among(plan["lows"] + plan["highs"])))
    def _():
        sigma = self_energy(own, beside, weights)
        sigma_out[0] = sigma[:size]
        sigma_out[1] = sigma[size:]


def second_kernel(plan, own, first, other, send):
    @pl.when(among(plan["mids"]))
    def _():
        sigma = [added(first[part], other[part]) for part in range(2)]
        put(send, stepped(own, *sigma))

    for members, source in ((plan["relayed"], other), (plan["late"], own)):

        @pl.when(among(members))
        def _():
            send[...] = source[...]


def middle_kernel(plan, below, above, sigma, out):
    @pl.when(among(plan["mids"]))
    def _():
        steps = [stepped(block, sigma[0], sigma[1]) for block in (below, above)]
        put(out, [added(*(step[part].astype(out.dtype) for step in steps)) for part in range(2)])


def neighbour_kernel(plan, first, second, third, middle, sigma, out):
    for members, source in ((plan["direct"], first), (plan["second_pairs"], second)):

        @pl.when(among(members))
        def _():
            put(out, stepped(source, sigma[0], sigma[1]))

    for members, source in (
        (plan["lows"], second),
        (plan["mids"], middle),
        (plan["highs"], third),
    ):

        @pl.when(among(members))
        def _():
            out[...] = source[...]


def last_kernel(plan, own, mine, other, weights, out):
    size = own.shape[-1]
    sigma = self_energy(mine, other, weights)
    put(out, stepped(own, sigma[:size], sigma[size:]))


LIMITS = pltpu.CompilerParams(vmem_limit_bytes=VMEM_LIMIT)
IN_VMEM = pl.BlockSpec(memory_space=pltpu.VMEM)
IN_HBM = pl.BlockSpec(memory_space=pltpu.HBM)


def like(block, space=jax.ShapeDtypeStruct):
    return space(block.shape, block.dtype)


def call(kernel, plan, *blocks):
    return pl.pallas_call(
        functools.partial(kernel, plan),
        out_shape=like(blocks[0]),
        in_specs=[IN_VMEM] * len(blocks),
        out_specs=IN_VMEM,
        compiler_params=LIMITS,
    )(*blocks)


def loaded(own, weights):
    return pl.pallas_call(
        load_kernel,
        out_shape=[like(own), like(weights)],
        in_specs=[IN_HBM] * 2,
        out_specs=[IN_VMEM] * 2,
        scratch_shapes=[pltpu.SemaphoreType.DMA((2,))],
        compiler_params=LIMITS,
        name="load_kernel",
    )(own, weights)


def first_sent(plan, own, beside, weights):
    return pl.pallas_call(
        functools.partial(first_kernel, plan),
        out_shape=like(own),
        in_specs=[IN_HBM, IN_VMEM, IN_HBM],
        out_specs=IN_VMEM,
        scratch_shapes=[
            (like(own, pltpu.VMEM), like(weights, pltpu.VMEM)),
            pltpu.SemaphoreType.DMA((2,)),
        ],
        compiler_params=LIMITS,
        name="first_kernel",
    )(own, beside, weights)


def chained(plan, green0, coupling):
    slabs = lax.axis_size("slab")
    everyone = range(lax.axis_size("energy"))
    outer = plan["lows"] + plan["highs"]

    def sent(value, flows):
        return lax.ppermute(value, "energy", plan[flows])

    def swapped(value, members):
        flows = [(e * slabs + s, e * slabs + slabs - 1 - s) for e in members for s in range(slabs)]
        return lax.ppermute(value, ("energy", "slab"), flows)

    far = pltpu.with_memory_space_constraint(green0[0, 0], pltpu.HBM)
    far_weights = pltpu.with_memory_space_constraint(coupling[0], pltpu.HBM)
    beside = swapped(green0[0, 0], outer)
    ends = sent(green0[0, 0], "ends")
    send = first_sent(plan, far, beside, far_weights)
    other, first = sent(send, "other"), sent(send, "first")
    own, weights = loaded(far, far_weights)
    beside = swapped(own, [e for e in everyone if e not in outer])
    above, below = sent(ends, "above"), sent(ends, "below")
    sigma = call(sigma_kernel, plan, own, beside, weights)
    send = call(second_kernel, plan, own, first, other)
    second, third = sent(send, "second"), sent(send, "third")
    middle = call(middle_kernel, plan, below, above, sigma)
    green = call(neighbour_kernel, plan, first, second, third, middle, sigma)
    out = call(last_kernel, plan, own, green, swapped(green, everyone), weights)
    return out[None, None]


def solution(mesh):
    plan = planned(mesh.shape["energy"]) if mesh.shape["slab"] == 2 else None
    local = functools.partial(chained, plan) if plan else plain
    placed = (P("energy", "slab", None, None, None), P("slab", None, None, None))
    return jax.shard_map(
        local,
        mesh=mesh,
        in_specs=placed,
        out_specs=P("energy", "slab", None, None, None),
        check_vma=False,
    )
```

```python
import functools

import jax
import jax.numpy as jnp
from jax import lax
from jax.experimental import pallas as pl
from jax.experimental.pallas import tpu as pltpu
from jax.sharding import PartitionSpec as P

OFFSET = 7
ITERS = 2
VMEM_LIMIT = 12 << 20
ROW, LAYER = 2, 4


def passed_along(value, axis, steps):
    count = lax.axis_size(axis)
    first, last = (max(0, -steps), min(count, count - steps))
    return lax.ppermute(value, axis, [(source, source + steps) for source in range(first, last)])


def with_halo(block, sides, width):
    for axis, dim in sides:
        count = lax.axis_size(axis)
        forward = [(i, i + 1) for i in range(count - 1)]
        backward = [(target, source) for source, target in forward]
        low = lax.ppermute(
            lax.slice_in_dim(block, block.shape[dim] - width, None, axis=dim), axis, forward
        )
        high = lax.ppermute(lax.slice_in_dim(block, 0, width, axis=dim), axis, backward)
        block = jnp.concatenate([low, block, high], axis=dim)
    return block


def dyson(green0, coupling, summed):
    count = green0.shape[1]
    size = green0.shape[-1]
    sigma = jnp.zeros(green0.shape, jnp.float32)
    for index in range(3):
        part = summed[:, index : index + count]
        weights = coupling[:, index]
        left = jnp.einsum(
            "sij,escjk->escik", weights, part, preferred_element_type=jnp.float32
        ).astype(jnp.bfloat16)
        sigma = sigma + jnp.einsum(
            "escij,skj->escik", left, weights, preferred_element_type=jnp.float32
        )
    sigma = sigma.astype(jnp.bfloat16)
    green_re = green0[:, :, 0]
    green_im = green0[:, :, 1]
    form = "esij,esjk->esik"
    prod_re = jnp.einsum(
        form, green_re, sigma[:, :, 0], preferred_element_type=jnp.float32
    ) - jnp.einsum(form, green_im, sigma[:, :, 1], preferred_element_type=jnp.float32)
    prod_im = jnp.einsum(
        form, green_re, sigma[:, :, 1], preferred_element_type=jnp.float32
    ) + jnp.einsum(form, green_im, sigma[:, :, 0], preferred_element_type=jnp.float32)
    prod_re = prod_re.astype(jnp.bfloat16)
    prod_im = prod_im.astype(jnp.bfloat16)
    trans = "esij,eskj->esik"
    out_re = jnp.einsum(trans, prod_re, green_re, preferred_element_type=jnp.float32) - jnp.einsum(
        trans, prod_im, green_im, preferred_element_type=jnp.float32
    )
    out_im = jnp.einsum(trans, prod_re, green_im, preferred_element_type=jnp.float32) + jnp.einsum(
        trans, prod_im, green_re, preferred_element_type=jnp.float32
    )
    result = green0.astype(jnp.float32) + jnp.stack([out_re, out_im], axis=2) / size
    return result.astype(jnp.bfloat16)


def plain(green0, coupling):
    green = green0
    for _ in range(ITERS):
        lower = passed_along(green, "energy", OFFSET)
        upper = passed_along(green, "energy", -OFFSET)
        own_sum = (lower.astype(jnp.float32) + upper.astype(jnp.float32)).astype(jnp.bfloat16)
        summed = with_halo(own_sum, (("slab", 1),), 1)
        green = dyson(green0, coupling, summed)
    return green


def links(source, target):
    passed, at = [], source
    for step, size in ((LAYER, None), (1, ROW), (ROW, LAYER)):
        here, there = ((e // step if size is None else e % size // step) for e in (at, target))
        for _ in range(abs(there - here)):
            to = at + (step if there > here else -step)
            passed.append((at, to))
            at = to
    return passed


def planned(energies):
    chains = [list(range(first, energies, OFFSET)) for first in range(min(OFFSET, energies))]
    threes = [chain for chain in chains if len(chain) == 3]
    twos = [chain for chain in chains if len(chain) == 2]
    if len(threes) != 2 or len(threes) + len(twos) != len(chains):
        return None
    (low0, mid0, high0), (low1, mid1, high1) = threes
    inward = [(low0, mid0), (low1, mid1), (high0, mid0), (high1, mid1)]
    plan = {
        "first": inward[:2],
        "other": inward[2:],
        "second": [(mid0, low0), (mid1, low1)],
        "third": [(mid0, high0), (mid1, high1)],
    }
    busy = {link for flow in inward for link in links(*flow)}
    taken = set()
    direct, late, relays = [], [], []
    for source, target in [flow for a, b in twos for flow in ((a, b), (b, a))]:
        passed = set(links(source, target))
        relay = target - target % LAYER + source % LAYER
        if passed & taken or any(abs(a - b) == LAYER for a, b in passed & busy):
            plan["second"].append((source, target))
            late.append((source, target))
        elif passed & busy:
            plan["other"].append((source, relay))
            plan["second"].append((relay, target))
            relays.append((relay, target))
            taken |= set(links(source, relay))
        else:
            plan["first"].append((source, target))
            direct.append(target)
            taken |= passed
    for flows in plan.values():
        sources, targets = zip(*flows)
        if len(set(sources)) < len(flows) or len(set(targets)) < len(flows):
            return None
    plan["lows"], plan["mids"], plan["highs"] = ([a, b] for a, b in zip(*threes))
    plan["direct"] = direct
    plan["relayed"] = [relay for relay, _ in relays]
    plan["late"] = [source for source, _ in late]
    plan["second_pairs"] = [target for _, target in late + relays]
    return plan


def dot(left, right):
    return jnp.dot(left, right, preferred_element_type=jnp.float32)


def dot_t(left, right):
    return lax.dot_general(
        left, right, (((1,), (1,)), ((), ())), preferred_element_type=jnp.float32
    )


def among(members):
    energy = lax.axis_index("energy")
    return functools.reduce(jnp.logical_or, [energy == member for member in members])


def half_energy(block, weight):
    size = block.shape[-1]
    left = dot(weight, jnp.concatenate([block[0], block[1]], axis=1)).astype(jnp.bfloat16)
    return dot_t(jnp.concatenate([left[:, :size], left[:, size:]], axis=0), weight)


def far_weight(weights):
    return weights[2 - 2 * lax.axis_index("slab")]


def self_energy(mine, other, weights):
    size = mine.shape[-1]
    own, far = weights[1], far_weight(weights)
    near = dot(own, jnp.concatenate([mine[0], mine[1]], axis=1)).astype(jnp.bfloat16)
    cross = dot(far, jnp.concatenate([other[0], other[1]], axis=1)).astype(jnp.bfloat16)
    left = jnp.concatenate(
        [
            jnp.concatenate([near[:, :size], cross[:, :size]], axis=1),
            jnp.concatenate([near[:, size:], cross[:, size:]], axis=1),
        ],
        axis=0,
    )
    return dot_t(left, jnp.concatenate([own, far], axis=1)).astype(jnp.bfloat16)


def stepped(green, sigma_re, sigma_im):
    re, im = green[0], green[1]
    size = re.shape[0]
    square = jnp.concatenate(
        [
            jnp.concatenate([sigma_re, sigma_im], axis=1),
            jnp.concatenate([-sigma_im, sigma_re], axis=1),
        ],
        axis=0,
    )
    product = dot(jnp.concatenate([re, im], axis=1), square).astype(jnp.bfloat16)
    turned = jnp.concatenate(
        [jnp.concatenate([re, -im], axis=1), jnp.concatenate([im, re], axis=1)], axis=0
    )
    added = dot_t(product, turned)
    return (
        re.astype(jnp.float32) + added[:, :size] / size,
        im.astype(jnp.float32) + added[:, size:] / size,
    )


def put(out, parts):
    for part, value in enumerate(parts):
        out[part] = value.astype(out.dtype)


def added(one, two):
    return (one.astype(jnp.float32) + two.astype(jnp.float32)).astype(one.dtype)


def load_kernel(own, weights, own_out, weights_out, sems):
    copies = [
        pltpu.make_async_copy(own, own_out, sems.at[0]),
        pltpu.make_async_copy(weights, weights_out, sems.at[1]),
    ]
    for copy in copies:
        copy.start()
    for copy in copies:
        copy.wait()


def sigma_kernel(plan, own, beside, weights, out):
    size = own.shape[-1]

    @pl.when(jnp.logical_not(among(plan["lows"] + plan["highs"])))
    def _():
        sigma = self_energy(own, beside, weights)
        out[0] = sigma[:size]
        out[1] = sigma[size:]


def sum_kernel(plan, first, other, out):
    @pl.when(among(plan["mids"]))
    def _():
        out[...] = added(first[...], other[...])


def near_kernel(plan, both, weights, out):
    @pl.when(among(plan["mids"]))
    def _():
        out[...] = half_energy(both, weights[1])


def second_kernel(plan, own, near, across, weights, other, send):
    @pl.when(among(plan["mids"]))
    def _():
        size = own.shape[-1]
        sigma = near[...] + half_energy(across, far_weight(weights))
        sigma = sigma.astype(jnp.bfloat16)
        put(send, stepped(own, sigma[:size], sigma[size:]))

    for members, source in ((plan["relayed"], other), (plan["late"], own)):

        @pl.when(among(members))
        def _():
            send[...] = source[...]


def middle_kernel(plan, first, other, sigma, out):
    @pl.when(among(plan["mids"]))
    def _():
        steps = [stepped(block, sigma[0], sigma[1]) for block in (first, other)]
        put(out, [added(*(step[part].astype(out.dtype) for step in steps)) for part in range(2)])


def neighbour_kernel(plan, first, second, third, middle, sigma, out):
    for members, source in ((plan["direct"], first), (plan["second_pairs"], second)):

        @pl.when(among(members))
        def _():
            put(out, stepped(source, sigma[0], sigma[1]))

    for members, source in (
        (plan["lows"], second),
        (plan["mids"], middle),
        (plan["highs"], third),
    ):

        @pl.when(among(members))
        def _():
            out[...] = source[...]


def close_kernel(plan, green, weights, out):
    out[...] = half_energy(green, weights[1])


def last_kernel(plan, own, near, across, weights, out):
    size = own.shape[-1]
    sigma = near[...] + half_energy(across, far_weight(weights))
    sigma = sigma.astype(jnp.bfloat16)
    put(out, stepped(own, sigma[:size], sigma[size:]))


LIMITS = pltpu.CompilerParams(vmem_limit_bytes=VMEM_LIMIT)
IN_VMEM = pl.BlockSpec(memory_space=pltpu.VMEM)
IN_HBM = pl.BlockSpec(memory_space=pltpu.HBM)


def like(block, space=jax.ShapeDtypeStruct):
    return space(block.shape, block.dtype)


def call(kernel, plan, *blocks, out=None):
    return pl.pallas_call(
        functools.partial(kernel, plan),
        out_shape=out or like(blocks[0]),
        in_specs=[IN_VMEM] * len(blocks),
        out_specs=IN_VMEM,
        compiler_params=LIMITS,
    )(*blocks)


def loaded(own, weights):
    return pl.pallas_call(
        load_kernel,
        out_shape=[like(own), like(weights)],
        in_specs=[IN_HBM] * 2,
        out_specs=[IN_VMEM] * 2,
        scratch_shapes=[pltpu.SemaphoreType.DMA((2,))],
        compiler_params=LIMITS,
        name="load_kernel",
    )(own, weights)


def chained(plan, green0, coupling):
    slabs = lax.axis_size("slab")
    everyone = range(lax.axis_size("energy"))
    size = green0.shape[-1]
    wide = jax.ShapeDtypeStruct((2 * size, size), jnp.float32)

    def sent(value, flows):
        return lax.ppermute(value, "energy", plan[flows])

    def swapped(value, members):
        flows = [(e * slabs + s, e * slabs + slabs - 1 - s) for e in members for s in range(slabs)]
        return lax.ppermute(value, ("energy", "slab"), flows)

    far = pltpu.with_memory_space_constraint(green0[0, 0], pltpu.HBM)
    far_weights = pltpu.with_memory_space_constraint(coupling[0], pltpu.HBM)
    first, other = sent(green0[0, 0], "first"), sent(green0[0, 0], "other")
    own, weights = loaded(far, far_weights)
    sigma = call(sigma_kernel, plan, own, swapped(own, everyone), weights)
    both = call(sum_kernel, plan, first, other)
    across = swapped(both, everyone)
    near = call(near_kernel, plan, both, weights, out=wide)
    send = call(second_kernel, plan, own, near, across, weights, other)
    second, third = sent(send, "second"), sent(send, "third")
    middle = call(middle_kernel, plan, first, other, sigma)
    green = call(neighbour_kernel, plan, first, second, third, middle, sigma)
    across = swapped(green, everyone)
    near = call(close_kernel, plan, green, weights, out=wide)
    out = call(last_kernel, plan, own, near, across, weights)
    return out[None, None]


def solution(mesh):
    plan = planned(mesh.shape["energy"]) if mesh.shape["slab"] == 2 else None
    local = functools.partial(chained, plan) if plan else plain
    placed = (P("energy", "slab", None, None, None), P("slab", None, None, None))
    return jax.shard_map(
        local,
        mesh=mesh,
        in_specs=placed,
        out_specs=P("energy", "slab", None, None, None),
        check_vma=False,
    )
```

```python
import functools

import jax
import jax.numpy as jnp
from jax import lax
from jax.experimental import pallas as pl
from jax.experimental.pallas import tpu as pltpu
from jax.sharding import PartitionSpec as P

OFFSET = 7
ITERS = 2
VMEM_LIMIT = 12 << 20
ROW, LAYER = 2, 4


def passed_along(value, axis, steps):
    count = lax.axis_size(axis)
    first, last = (max(0, -steps), min(count, count - steps))
    return lax.ppermute(value, axis, [(source, source + steps) for source in range(first, last)])


def with_halo(block, sides, width):
    for axis, dim in sides:
        count = lax.axis_size(axis)
        forward = [(i, i + 1) for i in range(count - 1)]
        backward = [(target, source) for source, target in forward]
        low = lax.ppermute(
            lax.slice_in_dim(block, block.shape[dim] - width, None, axis=dim), axis, forward
        )
        high = lax.ppermute(lax.slice_in_dim(block, 0, width, axis=dim), axis, backward)
        block = jnp.concatenate([low, block, high], axis=dim)
    return block


def dyson(green0, coupling, summed):
    count = green0.shape[1]
    size = green0.shape[-1]
    sigma = jnp.zeros(green0.shape, jnp.float32)
    for index in range(3):
        part = summed[:, index : index + count]
        weights = coupling[:, index]
        left = jnp.einsum(
            "sij,escjk->escik", weights, part, preferred_element_type=jnp.float32
        ).astype(jnp.bfloat16)
        sigma = sigma + jnp.einsum(
            "escij,skj->escik", left, weights, preferred_element_type=jnp.float32
        )
    sigma = sigma.astype(jnp.bfloat16)
    green_re = green0[:, :, 0]
    green_im = green0[:, :, 1]
    form = "esij,esjk->esik"
    prod_re = jnp.einsum(
        form, green_re, sigma[:, :, 0], preferred_element_type=jnp.float32
    ) - jnp.einsum(form, green_im, sigma[:, :, 1], preferred_element_type=jnp.float32)
    prod_im = jnp.einsum(
        form, green_re, sigma[:, :, 1], preferred_element_type=jnp.float32
    ) + jnp.einsum(form, green_im, sigma[:, :, 0], preferred_element_type=jnp.float32)
    prod_re = prod_re.astype(jnp.bfloat16)
    prod_im = prod_im.astype(jnp.bfloat16)
    trans = "esij,eskj->esik"
    out_re = jnp.einsum(trans, prod_re, green_re, preferred_element_type=jnp.float32) - jnp.einsum(
        trans, prod_im, green_im, preferred_element_type=jnp.float32
    )
    out_im = jnp.einsum(trans, prod_re, green_im, preferred_element_type=jnp.float32) + jnp.einsum(
        trans, prod_im, green_re, preferred_element_type=jnp.float32
    )
    result = green0.astype(jnp.float32) + jnp.stack([out_re, out_im], axis=2) / size
    return result.astype(jnp.bfloat16)


def plain(green0, coupling):
    green = green0
    for _ in range(ITERS):
        lower = passed_along(green, "energy", OFFSET)
        upper = passed_along(green, "energy", -OFFSET)
        own_sum = (lower.astype(jnp.float32) + upper.astype(jnp.float32)).astype(jnp.bfloat16)
        summed = with_halo(own_sum, (("slab", 1),), 1)
        green = dyson(green0, coupling, summed)
    return green


def links(source, target):
    passed, at = [], source
    for step, size in ((LAYER, None), (1, ROW), (ROW, LAYER)):
        here, there = ((e // step if size is None else e % size // step) for e in (at, target))
        for _ in range(abs(there - here)):
            to = at + (step if there > here else -step)
            passed.append((at, to))
            at = to
    return passed


def planned(energies):
    chains = [list(range(first, energies, OFFSET)) for first in range(min(OFFSET, energies))]
    threes = [chain for chain in chains if len(chain) == 3]
    twos = [chain for chain in chains if len(chain) == 2]
    if len(threes) != 2 or len(threes) + len(twos) != len(chains):
        return None
    (low0, mid0, high0), (low1, mid1, high1) = threes
    inward = [(low0, mid0), (low1, mid1), (high0, mid0), (high1, mid1)]
    plan = {
        "first": inward[:2],
        "other": inward[2:],
        "second": [(mid0, low0), (mid1, low1)],
        "third": [(mid0, high0), (mid1, high1)],
    }
    busy = {link for flow in inward for link in links(*flow)}
    taken = set()
    direct, late, relays = [], [], []
    for source, target in [flow for a, b in twos for flow in ((a, b), (b, a))]:
        passed = set(links(source, target))
        relay = target - target % LAYER + source % LAYER
        if passed & taken or any(abs(a - b) == LAYER for a, b in passed & busy):
            plan["second"].append((source, target))
            late.append((source, target))
        elif passed & busy:
            plan["first"].append((source, relay))
            plan["second"].append((relay, target))
            relays.append((relay, target))
            taken |= set(links(source, relay))
        else:
            direct.append((source, target))
            taken |= passed
    relayed = {relay for relay, _ in relays}
    plan["first"] += [flow for flow in direct if flow[1] not in relayed]
    plan["other"] += [flow for flow in direct if flow[1] in relayed]
    for flows in plan.values():
        sources, targets = zip(*flows)
        if len(set(sources)) < len(flows) or len(set(targets)) < len(flows):
            return None
    plan["lows"], plan["mids"], plan["highs"] = ([a, b] for a, b in zip(*threes))
    plan["direct"] = [target for _, target in direct if target in relayed]
    plan["early"] = [target for _, target in direct if target not in relayed]
    plan["relayed"] = [relay for relay, _ in relays]
    plan["late"] = [source for source, _ in late]
    plan["second_pairs"] = [target for _, target in late + relays]
    return plan


def dot(left, right):
    return jnp.dot(left, right, preferred_element_type=jnp.float32)


def dot_t(left, right):
    return lax.dot_general(
        left, right, (((1,), (1,)), ((), ())), preferred_element_type=jnp.float32
    )


def among(members):
    energy = lax.axis_index("energy")
    return functools.reduce(jnp.logical_or, [energy == member for member in members])


def far_weight(weights):
    return weights[2 - 2 * lax.axis_index("slab")]


def self_energy(mine, other, weights):
    size = mine.shape[-1]
    own, far = weights[1], far_weight(weights)
    near = dot(own, jnp.concatenate([mine[0], mine[1]], axis=1)).astype(jnp.bfloat16)
    cross = dot(far, jnp.concatenate([other[0], other[1]], axis=1)).astype(jnp.bfloat16)
    left = jnp.concatenate(
        [
            jnp.concatenate([near[:, :size], cross[:, :size]], axis=1),
            jnp.concatenate([near[:, size:], cross[:, size:]], axis=1),
        ],
        axis=0,
    )
    return dot_t(left, jnp.concatenate([own, far], axis=1)).astype(jnp.bfloat16)


def around(re, im, block_re, block_im):
    square = jnp.concatenate(
        [
            jnp.concatenate([block_re, block_im], axis=1),
            jnp.concatenate([-block_im, block_re], axis=1),
        ],
        axis=0,
    )
    product = dot(jnp.concatenate([re, im], axis=1), square).astype(jnp.bfloat16)
    turned = jnp.concatenate(
        [jnp.concatenate([re, -im], axis=1), jnp.concatenate([im, re], axis=1)], axis=0
    )
    return dot_t(product, turned)


def onto(green, added):
    size = added.shape[0]
    return [
        green[part].astype(jnp.float32) + added[:, part * size : (part + 1) * size] / size
        for part in range(2)
    ]


def stepped(green, sigma):
    return onto(green, around(green[0], green[1], sigma[0], sigma[1]))


def put(out, parts):
    for part, value in enumerate(parts):
        out[part] = value.astype(out.dtype)


def added(one, two):
    return (one.astype(jnp.float32) + two.astype(jnp.float32)).astype(one.dtype)


def load_kernel(own, weights, own_out, weights_out, sems):
    copies = [
        pltpu.make_async_copy(own, own_out, sems.at[0]),
        pltpu.make_async_copy(weights, weights_out, sems.at[1]),
    ]
    for copy in copies:
        copy.start()
    for copy in copies:
        copy.wait()


def sigma_kernel(plan, own, beside, weights, out):
    size = own.shape[-1]

    @pl.when(jnp.logical_not(among(plan["lows"] + plan["highs"])))
    def _():
        sigma = self_energy(own, beside, weights)
        out[0] = sigma[:size]
        out[1] = sigma[size:]


def sum_kernel(plan, first, other, out):
    @pl.when(among(plan["mids"]))
    def _():
        out[...] = added(first[...], other[...])


def turn_kernel(plan, own, weights, near, far):
    size = own.shape[-1]
    both = jnp.concatenate([weights[1], far_weight(weights)], axis=1)
    for part in range(2):
        turn = dot(own[part], both).astype(jnp.bfloat16)
        near[part] = turn[:, :size]
        far[part] = turn[:, size:]


def near_kernel(plan, turn, both, out):
    @pl.when(among(plan["mids"]))
    def _():
        out[...] = around(turn[0], turn[1], both[0], both[1])


def second_kernel(plan, own, turn, near, across, first, send):
    @pl.when(among(plan["mids"]))
    def _():
        put(send, onto(own, near[...] + around(turn[0], turn[1], across[0], across[1])))

    for members, source in ((plan["relayed"], first), (plan["late"], own)):

        @pl.when(among(members))
        def _():
            send[...] = source[...]


def middle_kernel(plan, first, other, sigma, out):
    @pl.when(among(plan["mids"]))
    def _():
        steps = [stepped(block, sigma) for block in (first, other)]
        put(out, [added(*(step[part].astype(out.dtype) for step in steps)) for part in range(2)])


def neighbour_kernel(plan, first, other, second, third, middle, sigma, out):
    for members, source in (
        (plan["early"], first),
        (plan["direct"], other),
        (plan["second_pairs"], second),
    ):

        @pl.when(among(members))
        def _():
            put(out, stepped(source, sigma))

    for members, source in (
        (plan["lows"], second),
        (plan["mids"], middle),
        (plan["highs"], third),
    ):

        @pl.when(among(members))
        def _():
            out[...] = source[...]


def close_kernel(plan, turn, green, out):
    out[...] = around(turn[0], turn[1], green[0], green[1])


def last_kernel(plan, own, turn, near, across, out):
    put(out, onto(own, near[...] + around(turn[0], turn[1], across[0], across[1])))


LIMITS = pltpu.CompilerParams(vmem_limit_bytes=VMEM_LIMIT)
IN_VMEM = pl.BlockSpec(memory_space=pltpu.VMEM)
IN_HBM = pl.BlockSpec(memory_space=pltpu.HBM)


def like(block, space=jax.ShapeDtypeStruct):
    return space(block.shape, block.dtype)


def call(kernel, plan, *blocks, out=None):
    return pl.pallas_call(
        functools.partial(kernel, plan),
        out_shape=out or like(blocks[0]),
        in_specs=[IN_VMEM] * len(blocks),
        out_specs=[IN_VMEM] * len(out) if isinstance(out, list) else IN_VMEM,
        compiler_params=LIMITS,
    )(*blocks)


def loaded(own, weights):
    return pl.pallas_call(
        load_kernel,
        out_shape=[like(own), like(weights)],
        in_specs=[IN_HBM] * 2,
        out_specs=[IN_VMEM] * 2,
        scratch_shapes=[pltpu.SemaphoreType.DMA((2,))],
        compiler_params=LIMITS,
        name="load_kernel",
    )(own, weights)


def chained(plan, green0, coupling):
    slabs = lax.axis_size("slab")
    everyone = range(lax.axis_size("energy"))
    size = green0.shape[-1]
    wide = jax.ShapeDtypeStruct((size, 2 * size), jnp.float32)

    def sent(value, flows):
        return lax.ppermute(value, "energy", plan[flows])

    def swapped(value, members):
        flows = [(e * slabs + s, e * slabs + slabs - 1 - s) for e in members for s in range(slabs)]
        return lax.ppermute(value, ("energy", "slab"), flows)

    far = pltpu.with_memory_space_constraint(green0[0, 0], pltpu.HBM)
    far_weights = pltpu.with_memory_space_constraint(coupling[0], pltpu.HBM)
    first, other = sent(green0[0, 0], "first"), sent(green0[0, 0], "other")
    own, weights = loaded(far, far_weights)
    sigma = call(sigma_kernel, plan, own, swapped(own, everyone), weights)
    near_turn, far_turn = call(turn_kernel, plan, own, weights, out=[like(own)] * 2)
    both = call(sum_kernel, plan, first, other)
    across = swapped(both, everyone)
    near = call(near_kernel, plan, near_turn, both, out=wide)
    send = call(second_kernel, plan, own, far_turn, near, across, first)
    second, third = sent(send, "second"), sent(send, "third")
    middle = call(middle_kernel, plan, first, other, sigma)
    green = call(neighbour_kernel, plan, first, other, second, third, middle, sigma)
    across = swapped(green, everyone)
    near = call(close_kernel, plan, near_turn, green, out=wide)
    out = call(last_kernel, plan, own, far_turn, near, across)
    return out[None, None]


def solution(mesh):
    plan = planned(mesh.shape["energy"]) if mesh.shape["slab"] == 2 else None
    local = functools.partial(chained, plan) if plan else plain
    placed = (P("energy", "slab", None, None, None), P("slab", None, None, None))
    return jax.shard_map(
        local,
        mesh=mesh,
        in_specs=placed,
        out_specs=P("energy", "slab", None, None, None),
        check_vma=False,
    )
```

```python
import functools

import jax
import jax.numpy as jnp
from jax import lax
from jax.experimental import pallas as pl
from jax.experimental.pallas import tpu as pltpu
from jax.sharding import PartitionSpec as P

OFFSET = 7
ITERS = 2
VMEM_LIMIT = 12 << 20
ROW, LAYER = 2, 4


def passed_along(value, axis, steps):
    count = lax.axis_size(axis)
    first, last = (max(0, -steps), min(count, count - steps))
    return lax.ppermute(value, axis, [(source, source + steps) for source in range(first, last)])


def with_halo(block, sides, width):
    for axis, dim in sides:
        count = lax.axis_size(axis)
        forward = [(i, i + 1) for i in range(count - 1)]
        backward = [(target, source) for source, target in forward]
        low = lax.ppermute(
            lax.slice_in_dim(block, block.shape[dim] - width, None, axis=dim), axis, forward
        )
        high = lax.ppermute(lax.slice_in_dim(block, 0, width, axis=dim), axis, backward)
        block = jnp.concatenate([low, block, high], axis=dim)
    return block


def dyson(green0, coupling, summed):
    count = green0.shape[1]
    size = green0.shape[-1]
    sigma = jnp.zeros(green0.shape, jnp.float32)
    for index in range(3):
        part = summed[:, index : index + count]
        weights = coupling[:, index]
        left = jnp.einsum(
            "sij,escjk->escik", weights, part, preferred_element_type=jnp.float32
        ).astype(jnp.bfloat16)
        sigma = sigma + jnp.einsum(
            "escij,skj->escik", left, weights, preferred_element_type=jnp.float32
        )
    sigma = sigma.astype(jnp.bfloat16)
    green_re = green0[:, :, 0]
    green_im = green0[:, :, 1]
    form = "esij,esjk->esik"
    prod_re = jnp.einsum(
        form, green_re, sigma[:, :, 0], preferred_element_type=jnp.float32
    ) - jnp.einsum(form, green_im, sigma[:, :, 1], preferred_element_type=jnp.float32)
    prod_im = jnp.einsum(
        form, green_re, sigma[:, :, 1], preferred_element_type=jnp.float32
    ) + jnp.einsum(form, green_im, sigma[:, :, 0], preferred_element_type=jnp.float32)
    prod_re = prod_re.astype(jnp.bfloat16)
    prod_im = prod_im.astype(jnp.bfloat16)
    trans = "esij,eskj->esik"
    out_re = jnp.einsum(trans, prod_re, green_re, preferred_element_type=jnp.float32) - jnp.einsum(
        trans, prod_im, green_im, preferred_element_type=jnp.float32
    )
    out_im = jnp.einsum(trans, prod_re, green_im, preferred_element_type=jnp.float32) + jnp.einsum(
        trans, prod_im, green_re, preferred_element_type=jnp.float32
    )
    result = green0.astype(jnp.float32) + jnp.stack([out_re, out_im], axis=2) / size
    return result.astype(jnp.bfloat16)


def plain(green0, coupling):
    green = green0
    for _ in range(ITERS):
        lower = passed_along(green, "energy", OFFSET)
        upper = passed_along(green, "energy", -OFFSET)
        own_sum = (lower.astype(jnp.float32) + upper.astype(jnp.float32)).astype(jnp.bfloat16)
        summed = with_halo(own_sum, (("slab", 1),), 1)
        green = dyson(green0, coupling, summed)
    return green


def links(source, target):
    passed, at = [], source
    for step, size in ((LAYER, None), (1, ROW), (ROW, LAYER)):
        here, there = ((e // step if size is None else e % size // step) for e in (at, target))
        for _ in range(abs(there - here)):
            to = at + (step if there > here else -step)
            passed.append((at, to))
            at = to
    return passed


def planned(energies):
    chains = [list(range(first, energies, OFFSET)) for first in range(min(OFFSET, energies))]
    threes = [chain for chain in chains if len(chain) == 3]
    twos = [chain for chain in chains if len(chain) == 2]
    if len(threes) != 2 or len(threes) + len(twos) != len(chains):
        return None
    (low0, mid0, high0), (low1, mid1, high1) = threes
    inward = [(low0, mid0), (low1, mid1), (high0, mid0), (high1, mid1)]
    plan = {
        "first": [],
        "other": [],
        "second": [],
        "inward_low": inward[:2],
        "inward_high": inward[2:],
        "back_low": [(mid0, low0), (mid1, low1)],
        "back_high": [(mid0, high0), (mid1, high1)],
    }
    busy = {link for flow in inward for link in links(*flow)}
    taken = set()
    direct, late, relays = [], [], []
    for source, target in [flow for a, b in twos for flow in ((a, b), (b, a))]:
        passed = set(links(source, target))
        relay = target - target % LAYER + source % LAYER
        if passed & taken or any(abs(a - b) == LAYER for a, b in passed & busy):
            plan["second"].append((source, target))
            late.append((source, target))
        elif passed & busy:
            plan["first"].append((source, relay))
            plan["second"].append((relay, target))
            relays.append((relay, target))
            taken |= set(links(source, relay))
        else:
            direct.append((source, target))
            taken |= passed
    relayed = {relay for relay, _ in relays}
    plan["first"] += [flow for flow in direct if flow[1] not in relayed]
    plan["other"] += [flow for flow in direct if flow[1] in relayed]
    for flows in plan.values():
        sources, targets = zip(*flows)
        if len(set(sources)) < len(flows) or len(set(targets)) < len(flows):
            return None
    plan["lows"], plan["mids"], plan["highs"] = ([a, b] for a, b in zip(*threes))
    plan["direct"] = [target for _, target in direct if target in relayed]
    plan["early"] = [target for _, target in direct if target not in relayed]
    plan["relayed"] = [relay for relay, _ in relays]
    plan["late"] = [source for source, _ in late]
    plan["second_pairs"] = [target for _, target in late + relays]
    return plan


def dot(left, right):
    return jnp.dot(left, right, preferred_element_type=jnp.float32)


def dot_t(left, right):
    return lax.dot_general(
        left, right, (((1,), (1,)), ((), ())), preferred_element_type=jnp.float32
    )


def among(members):
    energy = lax.axis_index("energy")
    return functools.reduce(jnp.logical_or, [energy == member for member in members])


def here(members, core):
    return jnp.logical_and(among(members), lax.axis_index("slab") == core)


def far_weight(weights):
    return weights[2 - 2 * lax.axis_index("slab")]


def self_energy(mine, other, weights):
    size = mine.shape[-1]
    own, far = weights[1], far_weight(weights)
    near = dot(own, jnp.concatenate([mine[0], mine[1]], axis=1)).astype(jnp.bfloat16)
    cross = dot(far, jnp.concatenate([other[0], other[1]], axis=1)).astype(jnp.bfloat16)
    left = jnp.concatenate(
        [
            jnp.concatenate([near[:, :size], cross[:, :size]], axis=1),
            jnp.concatenate([near[:, size:], cross[:, size:]], axis=1),
        ],
        axis=0,
    )
    return dot_t(left, jnp.concatenate([own, far], axis=1)).astype(jnp.bfloat16)


def around(re, im, block_re, block_im):
    square = jnp.concatenate(
        [
            jnp.concatenate([block_re, block_im], axis=1),
            jnp.concatenate([-block_im, block_re], axis=1),
        ],
        axis=0,
    )
    product = dot(jnp.concatenate([re, im], axis=1), square).astype(jnp.bfloat16)
    turned = jnp.concatenate(
        [jnp.concatenate([re, -im], axis=1), jnp.concatenate([im, re], axis=1)], axis=0
    )
    return dot_t(product, turned)


def onto(green, added):
    size = added.shape[0]
    return [
        green[part].astype(jnp.float32) + added[:, part * size : (part + 1) * size] / size
        for part in range(2)
    ]


def stepped(green, sigma):
    return onto(green, around(green[0], green[1], sigma[0], sigma[1]))


def put(out, parts):
    for part, value in enumerate(parts):
        out[part] = value.astype(out.dtype)


def added(one, two):
    return (one.astype(jnp.float32) + two.astype(jnp.float32)).astype(one.dtype)


def load_kernel(own, weights, own_out, weights_out, sems):
    copies = [
        pltpu.make_async_copy(own, own_out, sems.at[0]),
        pltpu.make_async_copy(weights, weights_out, sems.at[1]),
    ]
    for copy in copies:
        copy.start()
    for copy in copies:
        copy.wait()


def sigma_kernel(plan, own, beside, weights, out):
    size = own.shape[-1]

    @pl.when(jnp.logical_not(among(plan["lows"] + plan["highs"])))
    def _():
        sigma = self_energy(own, beside, weights)
        out[0] = sigma[:size]
        out[1] = sigma[size:]


def sum_kernel(plan, low, high, out, core):
    @pl.when(here(plan["mids"], core))
    def _():
        out[...] = added(low[...], high[...])


def turn_kernel(plan, own, weights, near, far):
    size = own.shape[-1]
    both = jnp.concatenate([weights[1], far_weight(weights)], axis=1)
    for part in range(2):
        turn = dot(own[part], both).astype(jnp.bfloat16)
        near[part] = turn[:, :size]
        far[part] = turn[:, size:]


def early_kernel(plan, near_turn, far_turn, both, across, out):
    @pl.when(here(plan["mids"], 0))
    def _():
        out[...] = around(near_turn[0], near_turn[1], both[0], both[1])

    @pl.when(here(plan["mids"], 1))
    def _():
        out[...] = around(far_turn[0], far_turn[1], across[0], across[1])


def second_kernel(plan, own, turn, near, both, first, send):
    @pl.when(here(plan["mids"], 1))
    def _():
        put(send, onto(own, near[...] + around(turn[0], turn[1], both[0], both[1])))

    for members, source in ((plan["relayed"], first), (plan["late"], own)):

        @pl.when(among(members))
        def _():
            send[...] = source[...]


def third_kernel(plan, own, turn, near, across, send):
    @pl.when(here(plan["mids"], 0))
    def _():
        put(send, onto(own, near[...] + around(turn[0], turn[1], across[0], across[1])))


def middle_kernel(plan, low0, high0, low1, high1, sigma, out):
    for core, blocks in enumerate(((low0, high0), (low1, high1))):

        @pl.when(here(plan["mids"], core))
        def _():
            steps = [stepped(block, sigma) for block in blocks]
            for part in range(2):
                out[part] = added(*(step[part].astype(out.dtype) for step in steps))


def neighbour_kernel(plan, first, other, second, low0, high0, low1, high1, middle, sigma, out):
    for members, source in (
        (plan["early"], first),
        (plan["direct"], other),
        (plan["second_pairs"], second),
    ):

        @pl.when(among(members))
        def _():
            put(out, stepped(source, sigma))

    ends = [
        (core, back[side], plan[members])
        for core, back in enumerate(((low0, high0), (low1, high1)))
        for side, members in enumerate(("lows", "highs"))
    ]
    for core, source, members in ends:

        @pl.when(here(members, core))
        def _():
            out[...] = source[...]

    @pl.when(among(plan["mids"]))
    def _():
        out[...] = middle[...]


def close_kernel(plan, turn, green, out):
    out[...] = around(turn[0], turn[1], green[0], green[1])


def last_kernel(plan, own, turn, near, across, out):
    put(out, onto(own, near[...] + around(turn[0], turn[1], across[0], across[1])))


LIMITS = pltpu.CompilerParams(vmem_limit_bytes=VMEM_LIMIT)
IN_VMEM = pl.BlockSpec(memory_space=pltpu.VMEM)
IN_HBM = pl.BlockSpec(memory_space=pltpu.HBM)


def like(block, space=jax.ShapeDtypeStruct):
    return space(block.shape, block.dtype)


def call(kernel, plan, *blocks, out=None, **options):
    return pl.pallas_call(
        functools.partial(kernel, plan, **options),
        out_shape=out or like(blocks[0]),
        in_specs=[IN_VMEM] * len(blocks),
        out_specs=[IN_VMEM] * len(out) if isinstance(out, list) else IN_VMEM,
        compiler_params=LIMITS,
    )(*blocks)


def loaded(own, weights):
    return pl.pallas_call(
        load_kernel,
        out_shape=[like(own), like(weights)],
        in_specs=[IN_HBM] * 2,
        out_specs=[IN_VMEM] * 2,
        scratch_shapes=[pltpu.SemaphoreType.DMA((2,))],
        compiler_params=LIMITS,
        name="load_kernel",
    )(own, weights)


def chained(plan, green0, coupling):
    slabs = lax.axis_size("slab")
    size = green0.shape[-1]
    wide = jax.ShapeDtypeStruct((size, 2 * size), jnp.float32)

    def sent(value, flows, cores=range(slabs)):
        pairs = [(a * slabs + s, b * slabs + s) for a, b in plan[flows] for s in cores]
        return lax.ppermute(value, ("energy", "slab"), pairs)

    def swapped(value):
        flows = [(s, slabs - 1 - s) for s in range(slabs)]
        return lax.ppermute(value, "slab", flows)

    def inward(value, core):
        return [sent(value, "inward_" + side, [core]) for side in SIDES]

    def back(value, core):
        return [sent(value, "back_" + side, [core]) for side in SIDES]

    given = green0[0, 0]
    far = pltpu.with_memory_space_constraint(given, pltpu.HBM)
    far_weights = pltpu.with_memory_space_constraint(coupling[0], pltpu.HBM)
    in0 = inward(given, 0)
    first, other = sent(given, "first"), sent(given, "other")
    own, weights = loaded(far, far_weights)
    in1 = inward(own, 1)
    sigma = call(sigma_kernel, plan, own, swapped(own), weights)
    near_turn, far_turn = call(turn_kernel, plan, own, weights, out=[like(own)] * 2)
    both = call(sum_kernel, plan, *in0, core=0)
    across = swapped(both)
    near = call(early_kernel, plan, near_turn, far_turn, both, across, out=wide)
    both = call(sum_kernel, plan, *in1, core=1)
    across = swapped(both)
    send = call(second_kernel, plan, own, near_turn, near, both, first)
    back1 = back(send, 1)
    second = sent(send, "second")
    send = call(third_kernel, plan, own, far_turn, near, across)
    back0 = back(send, 0)
    middle = call(middle_kernel, plan, *in0, *in1, sigma)
    green = call(neighbour_kernel, plan, first, other, second, *back0, *back1, middle, sigma)
    across = swapped(green)
    near = call(close_kernel, plan, near_turn, green, out=wide)
    out = call(last_kernel, plan, own, far_turn, near, across)
    return out[None, None]


SIDES = ("low", "high")


def solution(mesh):
    plan = planned(mesh.shape["energy"]) if mesh.shape["slab"] == 2 else None
    local = functools.partial(chained, plan) if plan else plain
    placed = (P("energy", "slab", None, None, None), P("slab", None, None, None))
    return jax.shard_map(
        local,
        mesh=mesh,
        in_specs=placed,
        out_specs=P("energy", "slab", None, None, None),
        check_vma=False,
    )
```

```python
import functools

import jax
import jax.numpy as jnp
from jax import lax
from jax.experimental import pallas as pl
from jax.experimental.pallas import tpu as pltpu
from jax.sharding import PartitionSpec as P

OFFSET = 7
ITERS = 2
VMEM_LIMIT = 12 << 20
ROW, LAYER = 2, 4


def passed_along(value, axis, steps):
    count = lax.axis_size(axis)
    first, last = (max(0, -steps), min(count, count - steps))
    return lax.ppermute(value, axis, [(source, source + steps) for source in range(first, last)])


def with_halo(block, sides, width):
    for axis, dim in sides:
        count = lax.axis_size(axis)
        forward = [(i, i + 1) for i in range(count - 1)]
        backward = [(target, source) for source, target in forward]
        low = lax.ppermute(
            lax.slice_in_dim(block, block.shape[dim] - width, None, axis=dim), axis, forward
        )
        high = lax.ppermute(lax.slice_in_dim(block, 0, width, axis=dim), axis, backward)
        block = jnp.concatenate([low, block, high], axis=dim)
    return block


def dyson(green0, coupling, summed):
    count = green0.shape[1]
    size = green0.shape[-1]
    sigma = jnp.zeros(green0.shape, jnp.float32)
    for index in range(3):
        part = summed[:, index : index + count]
        weights = coupling[:, index]
        left = jnp.einsum(
            "sij,escjk->escik", weights, part, preferred_element_type=jnp.float32
        ).astype(jnp.bfloat16)
        sigma = sigma + jnp.einsum(
            "escij,skj->escik", left, weights, preferred_element_type=jnp.float32
        )
    sigma = sigma.astype(jnp.bfloat16)
    green_re = green0[:, :, 0]
    green_im = green0[:, :, 1]
    form = "esij,esjk->esik"
    prod_re = jnp.einsum(
        form, green_re, sigma[:, :, 0], preferred_element_type=jnp.float32
    ) - jnp.einsum(form, green_im, sigma[:, :, 1], preferred_element_type=jnp.float32)
    prod_im = jnp.einsum(
        form, green_re, sigma[:, :, 1], preferred_element_type=jnp.float32
    ) + jnp.einsum(form, green_im, sigma[:, :, 0], preferred_element_type=jnp.float32)
    prod_re = prod_re.astype(jnp.bfloat16)
    prod_im = prod_im.astype(jnp.bfloat16)
    trans = "esij,eskj->esik"
    out_re = jnp.einsum(trans, prod_re, green_re, preferred_element_type=jnp.float32) - jnp.einsum(
        trans, prod_im, green_im, preferred_element_type=jnp.float32
    )
    out_im = jnp.einsum(trans, prod_re, green_im, preferred_element_type=jnp.float32) + jnp.einsum(
        trans, prod_im, green_re, preferred_element_type=jnp.float32
    )
    result = green0.astype(jnp.float32) + jnp.stack([out_re, out_im], axis=2) / size
    return result.astype(jnp.bfloat16)


def plain(green0, coupling):
    green = green0
    for _ in range(ITERS):
        lower = passed_along(green, "energy", OFFSET)
        upper = passed_along(green, "energy", -OFFSET)
        own_sum = (lower.astype(jnp.float32) + upper.astype(jnp.float32)).astype(jnp.bfloat16)
        summed = with_halo(own_sum, (("slab", 1),), 1)
        green = dyson(green0, coupling, summed)
    return green


def links(source, target):
    passed, at = [], source
    for step, size in ((LAYER, None), (1, ROW), (ROW, LAYER)):
        here, there = ((e // step if size is None else e % size // step) for e in (at, target))
        for _ in range(abs(there - here)):
            to = at + (step if there > here else -step)
            passed.append((at, to))
            at = to
    return passed


def planned(energies):
    chains = [list(range(first, energies, OFFSET)) for first in range(min(OFFSET, energies))]
    threes = [chain for chain in chains if len(chain) == 3]
    twos = [chain for chain in chains if len(chain) == 2]
    if len(threes) != 2 or len(threes) + len(twos) != len(chains):
        return None
    (low0, mid0, high0), (low1, mid1, high1) = threes
    inward = [(low0, mid0), (low1, mid1), (high0, mid0), (high1, mid1)]
    plan = {
        "first": [],
        "other": [],
        "second": [],
        "inward_low": inward[:2],
        "inward_high": inward[2:],
        "back_low": [(mid0, low0), (mid1, low1)],
        "back_high": [(mid0, high0), (mid1, high1)],
    }
    busy = {link for flow in inward for link in links(*flow)}
    taken = set()
    direct, late, relays = [], [], []
    for source, target in [flow for a, b in twos for flow in ((a, b), (b, a))]:
        passed = set(links(source, target))
        relay = target - target % LAYER + source % LAYER
        if passed & taken or any(abs(a - b) == LAYER for a, b in passed & busy):
            plan["second"].append((source, target))
            late.append((source, target))
        elif passed & busy:
            plan["first"].append((source, relay))
            plan["second"].append((relay, target))
            relays.append((relay, target))
            taken |= set(links(source, relay))
        else:
            direct.append((source, target))
            taken |= passed
    relayed = {relay for relay, _ in relays}
    plan["first"] += [flow for flow in direct if flow[1] not in relayed]
    plan["other"] += [flow for flow in direct if flow[1] in relayed]
    for flows in plan.values():
        sources, targets = zip(*flows)
        if len(set(sources)) < len(flows) or len(set(targets)) < len(flows):
            return None
    plan["lows"], plan["mids"], plan["highs"] = ([a, b] for a, b in zip(*threes))
    plan["direct"] = [target for _, target in direct if target in relayed]
    plan["early"] = [target for _, target in direct if target not in relayed]
    plan["relayed"] = [relay for relay, _ in relays]
    plan["late"] = [source for source, _ in late]
    plan["second_pairs"] = [target for _, target in late + relays]
    return plan


def dot(left, right):
    return jnp.dot(left, right, preferred_element_type=jnp.float32)


def dot_t(left, right):
    return lax.dot_general(
        left, right, (((1,), (1,)), ((), ())), preferred_element_type=jnp.float32
    )


def among(members):
    energy = lax.axis_index("energy")
    return functools.reduce(jnp.logical_or, [energy == member for member in members])


def here(members, core):
    return jnp.logical_and(among(members), lax.axis_index("slab") == core)


def far_weight(weights):
    return weights[2 - 2 * lax.axis_index("slab")]


def self_energy(mine, other, weights):
    size = mine.shape[-1]
    own, far = weights[1], far_weight(weights)
    near = dot(own, jnp.concatenate([mine[0], mine[1]], axis=1)).astype(jnp.bfloat16)
    cross = dot(far, jnp.concatenate([other[0], other[1]], axis=1)).astype(jnp.bfloat16)
    left = jnp.concatenate(
        [
            jnp.concatenate([near[:, :size], cross[:, :size]], axis=1),
            jnp.concatenate([near[:, size:], cross[:, size:]], axis=1),
        ],
        axis=0,
    )
    return dot_t(left, jnp.concatenate([own, far], axis=1)).astype(jnp.bfloat16)


def around_factors(re, im, block_re, block_im):
    square = jnp.concatenate(
        [
            jnp.concatenate([block_re, block_im], axis=1),
            jnp.concatenate([-block_im, block_re], axis=1),
        ],
        axis=0,
    )
    product = dot(jnp.concatenate([re, im], axis=1), square).astype(jnp.bfloat16)
    turned = jnp.concatenate(
        [jnp.concatenate([re, -im], axis=1), jnp.concatenate([im, re], axis=1)], axis=0
    )
    return product, turned


def around(re, im, block_re, block_im):
    return dot_t(*around_factors(re, im, block_re, block_im))


def onto(green, added):
    size = added.shape[0]
    return [
        green[part].astype(jnp.float32) + added[:, part * size : (part + 1) * size] / size
        for part in range(2)
    ]


def stepped(green, sigma):
    return onto(green, around(green[0], green[1], sigma[0], sigma[1]))


def put(out, parts):
    for part, value in enumerate(parts):
        out[part] = value.astype(out.dtype)


def added(one, two):
    return (one.astype(jnp.float32) + two.astype(jnp.float32)).astype(one.dtype)


def load_kernel(own, weights, own_out, weights_out, sems):
    copies = [
        pltpu.make_async_copy(own, own_out, sems.at[0]),
        pltpu.make_async_copy(weights, weights_out, sems.at[1]),
    ]
    for copy in copies:
        copy.start()
    for copy in copies:
        copy.wait()


def sigma_kernel(plan, own, beside, weights, out):
    size = own.shape[-1]

    @pl.when(jnp.logical_not(among(plan["lows"] + plan["highs"])))
    def _():
        sigma = self_energy(own, beside, weights)
        out[0] = sigma[:size]
        out[1] = sigma[size:]


def sum_kernel(plan, low, high, out, core):
    @pl.when(here(plan["mids"], core))
    def _():
        out[...] = added(low[...], high[...])


def turn_kernel(plan, own, weights, near, far):
    size = own.shape[-1]
    both = jnp.concatenate([weights[1], far_weight(weights)], axis=1)
    for part in range(2):
        turn = dot(own[part], both).astype(jnp.bfloat16)
        near[part] = turn[:, :size]
        far[part] = turn[:, size:]


def early_kernel(plan, near_turn, far_turn, both, across, out):
    @pl.when(here(plan["mids"], 0))
    def _():
        out[...] = around(near_turn[0], near_turn[1], both[0], both[1])

    @pl.when(here(plan["mids"], 1))
    def _():
        out[...] = around(far_turn[0], far_turn[1], across[0], across[1])


def second_kernel(plan, own, turn, near, both, first, send):
    @pl.when(here(plan["mids"], 1))
    def _():
        put(send, onto(own, near[...] + around(turn[0], turn[1], both[0], both[1])))

    for members, source in ((plan["relayed"], first), (plan["late"], own)):

        @pl.when(among(members))
        def _():
            send[...] = source[...]


def third_kernel(plan, own, turn, near, across, send):
    @pl.when(here(plan["mids"], 0))
    def _():
        put(send, onto(own, near[...] + around(turn[0], turn[1], across[0], across[1])))


def middle_kernel(plan, low0, high0, low1, high1, sigma, out):
    for core, blocks in enumerate(((low0, high0), (low1, high1))):

        @pl.when(here(plan["mids"], core))
        def _():
            steps = [stepped(block, sigma) for block in blocks]
            for part in range(2):
                out[part] = added(*(step[part].astype(out.dtype) for step in steps))


def neighbour_kernel(plan, first, other, second, low0, high0, low1, high1, middle, sigma, out):
    for members, source in (
        (plan["early"], first),
        (plan["direct"], other),
        (plan["second_pairs"], second),
    ):

        @pl.when(among(members))
        def _():
            put(out, stepped(source, sigma))

    ends = [
        (core, back[side], plan[members])
        for core, back in enumerate(((low0, high0), (low1, high1)))
        for side, members in enumerate(("lows", "highs"))
    ]
    for core, source, members in ends:

        @pl.when(here(members, core))
        def _():
            out[...] = source[...]

    @pl.when(among(plan["mids"]))
    def _():
        out[...] = middle[...]


def close_kernel(plan, turn, green, out):
    out[...] = around(turn[0], turn[1], green[0], green[1])


def last_kernel(own, turn, near, across, out, held, sems):
    size = own.shape[-1]
    split = pl.cdiv(4 * size, 3)
    product, turned = around_factors(turn[0], turn[1], across[0], across[1])
    copies = [pltpu.make_async_copy(held.at[part], out.at[part], sems.at[part]) for part in (0, 1)]

    def close(part, columns, added):
        first = part * size + columns.start
        green = own[part][:, columns].astype(jnp.float32)
        total = near[:, first : first + added.shape[1]] + added
        held[part, :, columns] = (green + total / size).astype(held.dtype)

    added = dot_t(product, turned[:split])
    close(0, slice(0, size), added[:, :size])
    copies[0].start()
    close(1, slice(0, split - size), added[:, size:])
    close(1, slice(split - size, size), dot_t(product, turned[split:]))
    copies[1].start()
    for copy in copies:
        copy.wait()


LIMITS = pltpu.CompilerParams(vmem_limit_bytes=VMEM_LIMIT)
IN_VMEM = pl.BlockSpec(memory_space=pltpu.VMEM)
IN_HBM = pl.BlockSpec(memory_space=pltpu.HBM)


def like(block, space=jax.ShapeDtypeStruct):
    return space(block.shape, block.dtype)


def call(kernel, plan, *blocks, out=None, **options):
    return pl.pallas_call(
        functools.partial(kernel, plan, **options),
        out_shape=out or like(blocks[0]),
        in_specs=[IN_VMEM] * len(blocks),
        out_specs=[IN_VMEM] * len(out) if isinstance(out, list) else IN_VMEM,
        compiler_params=LIMITS,
    )(*blocks)


def ended(own, *blocks):
    return pl.pallas_call(
        last_kernel,
        out_shape=like(own),
        in_specs=[IN_VMEM] * (1 + len(blocks)),
        out_specs=IN_HBM,
        scratch_shapes=[like(own, pltpu.VMEM), pltpu.SemaphoreType.DMA((2,))],
        compiler_params=LIMITS,
        name="last_kernel",
    )(own, *blocks)


def loaded(own, weights):
    return pl.pallas_call(
        load_kernel,
        out_shape=[like(own), like(weights)],
        in_specs=[IN_HBM] * 2,
        out_specs=[IN_VMEM] * 2,
        scratch_shapes=[pltpu.SemaphoreType.DMA((2,))],
        compiler_params=LIMITS,
        name="load_kernel",
    )(own, weights)


def chained(plan, green0, coupling):
    slabs = lax.axis_size("slab")
    size = green0.shape[-1]
    wide = jax.ShapeDtypeStruct((size, 2 * size), jnp.float32)

    def sent(value, flows, cores=range(slabs)):
        pairs = [(a * slabs + s, b * slabs + s) for a, b in plan[flows] for s in cores]
        return lax.ppermute(value, ("energy", "slab"), pairs)

    def swapped(value):
        flows = [(s, slabs - 1 - s) for s in range(slabs)]
        return lax.ppermute(value, "slab", flows)

    def inward(value, core):
        return [sent(value, "inward_" + side, [core]) for side in SIDES]

    def back(value, core):
        return [sent(value, "back_" + side, [core]) for side in SIDES]

    given = green0[0, 0]
    far = pltpu.with_memory_space_constraint(given, pltpu.HBM)
    far_weights = pltpu.with_memory_space_constraint(coupling[0], pltpu.HBM)
    in0 = inward(given, 0)
    first, other = sent(given, "first"), sent(given, "other")
    own, weights = loaded(far, far_weights)
    in1 = inward(own, 1)
    sigma = call(sigma_kernel, plan, own, swapped(own), weights)
    near_turn, far_turn = call(turn_kernel, plan, own, weights, out=[like(own)] * 2)
    both = call(sum_kernel, plan, *in0, core=0)
    across = swapped(both)
    near = call(early_kernel, plan, near_turn, far_turn, both, across, out=wide)
    both = call(sum_kernel, plan, *in1, core=1)
    across = swapped(both)
    send = call(second_kernel, plan, own, near_turn, near, both, first)
    back1 = back(send, 1)
    second = sent(send, "second")
    send = call(third_kernel, plan, own, far_turn, near, across)
    back0 = back(send, 0)
    middle = call(middle_kernel, plan, *in0, *in1, sigma)
    green = call(neighbour_kernel, plan, first, other, second, *back0, *back1, middle, sigma)
    across = swapped(green)
    near = call(close_kernel, plan, near_turn, green, out=wide)
    out = ended(own, far_turn, near, across)
    return out[None, None]


SIDES = ("low", "high")


def solution(mesh):
    plan = planned(mesh.shape["energy"]) if mesh.shape["slab"] == 2 else None
    local = functools.partial(chained, plan) if plan else plain
    placed = (P("energy", "slab", None, None, None), P("slab", None, None, None))
    return jax.shard_map(
        local,
        mesh=mesh,
        in_specs=placed,
        out_specs=P("energy", "slab", None, None, None),
        check_vma=False,
    )
```

```python
import functools

import jax
import jax.numpy as jnp
from jax import lax
from jax.experimental import pallas as pl
from jax.experimental.pallas import tpu as pltpu
from jax.sharding import PartitionSpec as P

OFFSET = 7
ITERS = 2
VMEM_LIMIT = 12 << 20
ROW, LAYER = 2, 4


def passed_along(value, axis, steps):
    count = lax.axis_size(axis)
    first, last = (max(0, -steps), min(count, count - steps))
    return lax.ppermute(value, axis, [(source, source + steps) for source in range(first, last)])


def with_halo(block, sides, width):
    for axis, dim in sides:
        count = lax.axis_size(axis)
        forward = [(i, i + 1) for i in range(count - 1)]
        backward = [(target, source) for source, target in forward]
        low = lax.ppermute(
            lax.slice_in_dim(block, block.shape[dim] - width, None, axis=dim), axis, forward
        )
        high = lax.ppermute(lax.slice_in_dim(block, 0, width, axis=dim), axis, backward)
        block = jnp.concatenate([low, block, high], axis=dim)
    return block


def dyson(green0, coupling, summed):
    count = green0.shape[1]
    size = green0.shape[-1]
    sigma = jnp.zeros(green0.shape, jnp.float32)
    for index in range(3):
        part = summed[:, index : index + count]
        weights = coupling[:, index]
        left = jnp.einsum(
            "sij,escjk->escik", weights, part, preferred_element_type=jnp.float32
        ).astype(jnp.bfloat16)
        sigma = sigma + jnp.einsum(
            "escij,skj->escik", left, weights, preferred_element_type=jnp.float32
        )
    sigma = sigma.astype(jnp.bfloat16)
    green_re = green0[:, :, 0]
    green_im = green0[:, :, 1]
    form = "esij,esjk->esik"
    prod_re = jnp.einsum(
        form, green_re, sigma[:, :, 0], preferred_element_type=jnp.float32
    ) - jnp.einsum(form, green_im, sigma[:, :, 1], preferred_element_type=jnp.float32)
    prod_im = jnp.einsum(
        form, green_re, sigma[:, :, 1], preferred_element_type=jnp.float32
    ) + jnp.einsum(form, green_im, sigma[:, :, 0], preferred_element_type=jnp.float32)
    prod_re = prod_re.astype(jnp.bfloat16)
    prod_im = prod_im.astype(jnp.bfloat16)
    trans = "esij,eskj->esik"
    out_re = jnp.einsum(trans, prod_re, green_re, preferred_element_type=jnp.float32) - jnp.einsum(
        trans, prod_im, green_im, preferred_element_type=jnp.float32
    )
    out_im = jnp.einsum(trans, prod_re, green_im, preferred_element_type=jnp.float32) + jnp.einsum(
        trans, prod_im, green_re, preferred_element_type=jnp.float32
    )
    result = green0.astype(jnp.float32) + jnp.stack([out_re, out_im], axis=2) / size
    return result.astype(jnp.bfloat16)


def plain(green0, coupling):
    green = green0
    for _ in range(ITERS):
        lower = passed_along(green, "energy", OFFSET)
        upper = passed_along(green, "energy", -OFFSET)
        own_sum = (lower.astype(jnp.float32) + upper.astype(jnp.float32)).astype(jnp.bfloat16)
        summed = with_halo(own_sum, (("slab", 1),), 1)
        green = dyson(green0, coupling, summed)
    return green


def links(source, target):
    passed, at = [], source
    for step, size in ((LAYER, None), (1, ROW), (ROW, LAYER)):
        here, there = ((e // step if size is None else e % size // step) for e in (at, target))
        for _ in range(abs(there - here)):
            to = at + (step if there > here else -step)
            passed.append((at, to))
            at = to
    return passed


def planned(energies):
    chains = [list(range(first, energies, OFFSET)) for first in range(min(OFFSET, energies))]
    threes = [chain for chain in chains if len(chain) == 3]
    twos = [chain for chain in chains if len(chain) == 2]
    if len(threes) != 2 or len(threes) + len(twos) != len(chains):
        return None
    (low0, mid0, high0), (low1, mid1, high1) = threes
    inward = [(low0, mid0), (low1, mid1), (high0, mid0), (high1, mid1)]
    plan = {
        "first": [],
        "other": [],
        "second": [],
        "inward_low": inward[:2],
        "inward_high": inward[2:],
        "back_low": [(mid0, low0), (mid1, low1)],
        "back_high": [(mid0, high0), (mid1, high1)],
    }
    busy = {link for flow in inward for link in links(*flow)}
    taken = set()
    direct, late, relays = [], [], []
    for source, target in [flow for a, b in twos for flow in ((a, b), (b, a))]:
        passed = set(links(source, target))
        relay = target - target % LAYER + source % LAYER
        if passed & taken or any(abs(a - b) == LAYER for a, b in passed & busy):
            plan["second"].append((source, target))
            late.append((source, target))
        elif passed & busy:
            plan["first"].append((source, relay))
            plan["second"].append((relay, target))
            relays.append((relay, target))
            taken |= set(links(source, relay))
        else:
            direct.append((source, target))
            taken |= passed
    relayed = {relay for relay, _ in relays}
    plan["first"] += [flow for flow in direct if flow[1] not in relayed]
    plan["other"] += [flow for flow in direct if flow[1] in relayed]
    for flows in plan.values():
        sources, targets = zip(*flows)
        if len(set(sources)) < len(flows) or len(set(targets)) < len(flows):
            return None
    plan["lows"], plan["mids"], plan["highs"] = ([a, b] for a, b in zip(*threes))
    plan["direct"] = [target for _, target in direct if target in relayed]
    plan["early"] = [target for _, target in direct if target not in relayed]
    plan["relayed"] = [relay for relay, _ in relays]
    plan["late"] = [source for source, _ in late]
    plan["second_pairs"] = [target for _, target in late + relays]
    return plan


def dot(left, right):
    return jnp.dot(left, right, preferred_element_type=jnp.float32)


def dot_t(left, right):
    return lax.dot_general(
        left, right, (((1,), (1,)), ((), ())), preferred_element_type=jnp.float32
    )


def among(members):
    energy = lax.axis_index("energy")
    return functools.reduce(jnp.logical_or, [energy == member for member in members])


def here(members, core):
    return jnp.logical_and(among(members), lax.axis_index("slab") == core)


def far_weight(weights):
    return weights[2 - 2 * lax.axis_index("slab")]


def self_energy(mine, other, weights):
    size = mine.shape[-1]
    own, far = weights[1], far_weight(weights)
    near = dot(own, jnp.concatenate([mine[0], mine[1]], axis=1)).astype(jnp.bfloat16)
    cross = dot(far, jnp.concatenate([other[0], other[1]], axis=1)).astype(jnp.bfloat16)
    left = jnp.concatenate(
        [
            jnp.concatenate([near[:, :size], cross[:, :size]], axis=1),
            jnp.concatenate([near[:, size:], cross[:, size:]], axis=1),
        ],
        axis=0,
    )
    return dot_t(left, jnp.concatenate([own, far], axis=1)).astype(jnp.bfloat16)


def first_product(turn, block, first=0):
    columns = slice(first, first + block.shape[1])
    square = jnp.concatenate(
        [
            jnp.concatenate([block[0], block[1]], axis=1),
            jnp.concatenate([-block[1], block[0]], axis=1),
        ],
        axis=0,
    )
    return dot(jnp.concatenate([turn[0][:, columns], turn[1][:, columns]], axis=1), square)


def second_product(product, turn):
    re, im = turn[0], turn[1]
    turned = jnp.concatenate(
        [jnp.concatenate([re, -im], axis=1), jnp.concatenate([im, re], axis=1)], axis=0
    )
    return dot_t(product.astype(jnp.bfloat16), turned)


def around(turn, block):
    return second_product(first_product(turn, block), turn)


def onto(green, added):
    size = added.shape[0]
    return [
        green[part].astype(jnp.float32) + added[:, part * size : (part + 1) * size] / size
        for part in range(2)
    ]


def stepped(green, sigma):
    return onto(green, around(green, sigma))


def put(out, parts):
    for part, value in enumerate(parts):
        out[part] = value.astype(out.dtype)


def added(one, two):
    return (one.astype(jnp.float32) + two.astype(jnp.float32)).astype(one.dtype)


def load_kernel(own, weights, own_out, weights_out, sems):
    copies = [
        pltpu.make_async_copy(own, own_out, sems.at[0]),
        pltpu.make_async_copy(weights, weights_out, sems.at[1]),
    ]
    for copy in copies:
        copy.start()
    for copy in copies:
        copy.wait()


def sigma_kernel(plan, own, beside, weights, out):
    size = own.shape[-1]

    @pl.when(jnp.logical_not(among(plan["lows"] + plan["highs"])))
    def _():
        sigma = self_energy(own, beside, weights)
        out[0] = sigma[:size]
        out[1] = sigma[size:]


def sum_kernel(plan, low, high, out, core):
    @pl.when(here(plan["mids"], core))
    def _():
        out[...] = added(low[...], high[...])


def turn_kernel(plan, own, weights, near, far):
    size = own.shape[-1]
    both = jnp.concatenate([weights[1], far_weight(weights)], axis=1)
    for part in range(2):
        turn = dot(own[part], both).astype(jnp.bfloat16)
        near[part] = turn[:, :size]
        far[part] = turn[:, size:]


def early_kernel(plan, near_turn, far_turn, both, across, out):
    @pl.when(here(plan["mids"], 0))
    def _():
        out[...] = around(near_turn, both)

    @pl.when(here(plan["mids"], 1))
    def _():
        out[...] = around(far_turn, across)


def second_kernel(plan, own, turn, near, both, first, send):
    @pl.when(here(plan["mids"], 1))
    def _():
        put(send, onto(own, near[...] + around(turn, both)))

    for members, source in ((plan["relayed"], first), (plan["late"], own)):

        @pl.when(among(members))
        def _():
            send[...] = source[...]


def put_cut(head, tail, parts):
    cut = head.shape[1]
    for part in range(2):
        value = parts[part].astype(head.dtype)
        head[part] = value[:cut]
        tail[part] = value[cut:]


def third_kernel(plan, own, turn, near, across, head, tail):
    @pl.when(here(plan["mids"], 0))
    def _():
        put_cut(head, tail, onto(own, near[...] + around(turn, across)))


def middle_kernel(plan, low0, high0, low1, high1, sigma, out):
    for core, blocks in enumerate(((low0, high0), (low1, high1))):

        @pl.when(here(plan["mids"], core))
        def _():
            steps = [stepped(block, sigma) for block in blocks]
            for part in range(2):
                out[part] = added(*(step[part].astype(out.dtype) for step in steps))


def neighbour_kernel(
    plan, first, other, second, low0, high0, low1, high1, middle, sigma, head, tail
):
    for members, source in (
        (plan["early"], first),
        (plan["direct"], other),
        (plan["second_pairs"], second),
    ):

        @pl.when(among(members))
        def _():
            put_cut(head, tail, stepped(source, sigma))

    for members, source in ((plan["lows"], low0), (plan["highs"], high0)):

        @pl.when(here(members, 0))
        def _():
            head[...] = source[...]

    for members, source in ((plan["lows"], low1), (plan["highs"], high1)):

        @pl.when(here(members, 1))
        def _():
            put_cut(head, tail, source)

    @pl.when(among(plan["mids"]))
    def _():
        put_cut(head, tail, middle)


def tail_kernel(plan, made, low, high, out):
    is_low, is_high = here(plan["lows"], 0), here(plan["highs"], 0)

    @pl.when(jnp.logical_not(jnp.logical_or(is_low, is_high)))
    def _():
        out[...] = made[...]

    for is_here, source in ((is_low, low), (is_high, high)):

        @pl.when(is_here)
        def _():
            out[...] = source[...]


def head_kernel(plan, near_turn, far_turn, mine, across, near, far):
    near[...] = first_product(near_turn, mine)
    far[...] = first_product(far_turn, across)


def close_kernel(plan, turn, product, tail, out, cut):
    out[...] = second_product(product[...] + first_product(turn, tail, cut), turn)


def last_kernel(plan, own, turn, near, product, tail, out, cut):
    total = near[...] + second_product(product[...] + first_product(turn, tail, cut), turn)
    put(out, onto(own, total))


LIMITS = pltpu.CompilerParams(vmem_limit_bytes=VMEM_LIMIT)
IN_VMEM = pl.BlockSpec(memory_space=pltpu.VMEM)
IN_HBM = pl.BlockSpec(memory_space=pltpu.HBM)


def like(block, space=jax.ShapeDtypeStruct):
    return space(block.shape, block.dtype)


def call(kernel, plan, *blocks, out=None, **options):
    return pl.pallas_call(
        functools.partial(kernel, plan, **options),
        out_shape=out or like(blocks[0]),
        in_specs=[IN_VMEM] * len(blocks),
        out_specs=[IN_VMEM] * len(out) if isinstance(out, list) else IN_VMEM,
        compiler_params=LIMITS,
    )(*blocks)


def loaded(own, weights):
    return pl.pallas_call(
        load_kernel,
        out_shape=[like(own), like(weights)],
        in_specs=[IN_HBM] * 2,
        out_specs=[IN_VMEM] * 2,
        scratch_shapes=[pltpu.SemaphoreType.DMA((2,))],
        compiler_params=LIMITS,
        name="load_kernel",
    )(own, weights)


def chained(plan, green0, coupling):
    slabs = lax.axis_size("slab")
    size = green0.shape[-1]
    wide = jax.ShapeDtypeStruct((size, 2 * size), jnp.float32)
    cut = size - size // 3
    cut_shapes = [
        jax.ShapeDtypeStruct((2, rows, size), green0.dtype) for rows in (cut, size - cut)
    ]

    def sent(value, flows, cores=range(slabs)):
        pairs = [(a * slabs + s, b * slabs + s) for a, b in plan[flows] for s in cores]
        return lax.ppermute(value, ("energy", "slab"), pairs)

    def swapped(value):
        flows = [(s, slabs - 1 - s) for s in range(slabs)]
        return lax.ppermute(value, "slab", flows)

    def inward(value, core):
        return [sent(value, "inward_" + side, [core]) for side in SIDES]

    def back(value, core):
        return [sent(value, "back_" + side, [core]) for side in SIDES]

    given = green0[0, 0]
    far = pltpu.with_memory_space_constraint(given, pltpu.HBM)
    far_weights = pltpu.with_memory_space_constraint(coupling[0], pltpu.HBM)
    in0 = inward(given, 0)
    first, other = sent(given, "first"), sent(given, "other")
    own, weights = loaded(far, far_weights)
    in1 = inward(own, 1)
    sigma = call(sigma_kernel, plan, own, swapped(own), weights)
    near_turn, far_turn = call(turn_kernel, plan, own, weights, out=[like(own)] * 2)
    both = call(sum_kernel, plan, *in0, core=0)
    across = swapped(both)
    near = call(early_kernel, plan, near_turn, far_turn, both, across, out=wide)
    both = call(sum_kernel, plan, *in1, core=1)
    across = swapped(both)
    send = call(second_kernel, plan, own, near_turn, near, both, first)
    back1 = back(send, 1)
    second = sent(send, "second")
    head, tail = call(third_kernel, plan, own, far_turn, near, across, out=cut_shapes)
    heads, tails = back(head, 0), back(tail, 0)
    middle = call(middle_kernel, plan, *in0, *in1, sigma)
    head, tail = call(
        neighbour_kernel, plan, first, other, second, *heads, *back1, middle, sigma, out=cut_shapes
    )
    across = swapped(head)
    near, far_product = call(
        head_kernel, plan, near_turn, far_turn, head, across, out=[wide, wide]
    )
    tail = call(tail_kernel, plan, tail, *tails)
    across = swapped(tail)
    near = call(close_kernel, plan, near_turn, near, tail, out=wide, cut=cut)
    out = call(
        last_kernel, plan, own, far_turn, near, far_product, across, out=like(own), cut=cut
    )
    return out[None, None]


SIDES = ("low", "high")


def solution(mesh):
    plan = planned(mesh.shape["energy"]) if mesh.shape["slab"] == 2 else None
    local = functools.partial(chained, plan) if plan else plain
    placed = (P("energy", "slab", None, None, None), P("slab", None, None, None))
    return jax.shard_map(
        local,
        mesh=mesh,
        in_specs=placed,
        out_specs=P("energy", "slab", None, None, None),
        check_vma=False,
    )
```
